512 devices in a mesh: ta: 8 (over y_lo, core), gx: 8 (over y_hi, x), gy: 8 (over z).
Axes of the slice: x: 4, y: 8 (y_hi: 2, y_lo: 4; y = y_hi * 4 + y_lo), z: 8, core: 2. Of those that a mesh axis runs over, the one named last changes fastest.
Arguments:
- density: float32 [64, 512, 1024], P('ta', 'gx', 'gy'), may hold values from 0.25 to 9.5
- flux_x: float32 [64, 512, 1024], P('ta', 'gx', 'gy'), may hold values from -14 to 14
- flux_y: float32 [64, 512, 1024], P('ta', 'gx', 'gy'), may hold values from -14 to 14
- congestion: float32 [64, 512, 1024], P('ta', 'gx', 'gy'), may hold values from 0.2 to 5
- initial_density: float32 [512, 1024], P('gx', 'gy'), may hold values from 0.25 to 2.5
Outputs:
- mass_out: float32 [64, 512, 1024], P('ta', 'gx', 'gy')
- flux_x_out: float32 [64, 512, 1024], P('ta', 'gx', 'gy')
- flux_y_out: float32 [64, 512, 1024], P('ta', 'gx', 'gy')
The draws below stay inside these ranges and needn't reach their ends.
All inputs are finite; a program needn't handle non-finite values.
Results may differ from the reference program's by a relative error of at most 0.0003.
Values sent between devices are 32-bit elements; how exact they have to be, the bound alone decides.
A program may use at most 64 MiB of HBM per device.

```python
import math
import jax
import jax.numpy as jnp

CY = 128
ITERS = 3
NEWTON = 6
NT = 64
NX = 512
NY = 1024


def time_ramp():
    return (1.0 + 2.0 * jnp.arange(NT, dtype=jnp.float32) / NT)[:, None, None]


def block_levels(key, low_end, high_end):
    levels = jnp.exp(jax.random.uniform(key, (NY // CY,), jnp.float32, math.log(low_end), math.log(high_end)))
    return jnp.repeat(levels, CY).reshape(1, 1, NY)


def draw_density(key, part):
    base_vals = jax.random.uniform(key, (NT, NX, NY), jnp.float32, 0.25, 2.5)
    return base_vals * time_ramp()


def momentum_draw(key, length, wave_shape):
    rough_level = block_levels(jax.random.fold_in(key, 3), 0.3, 2.9)
    wave_level = block_levels(jax.random.fold_in(key, 5), 0.1, 1.0)
    phase = jax.random.uniform(jax.random.fold_in(key, 9), (NT, 1, 1), jnp.float32, -math.pi, math.pi)
    position = jnp.arange(length, dtype=jnp.float32).reshape(wave_shape)
    wave = jnp.sin(2.0 * math.pi * position / 16.0 + phase) * wave_level
    base_vals = jax.random.truncated_normal(key, -1.2, 1.2, (NT, NX, NY), jnp.float32)
    return (base_vals * rough_level + wave) * time_ramp()


def draw_flux_x(key, part):
    return momentum_draw(jax.random.fold_in(key, 11), NX, (1, NX, 1))


def draw_flux_y(key, part):
    return momentum_draw(jax.random.fold_in(key, 13), NY, (1, 1, NY))


def block_scale(rng, shape, cuts, smallest, high):
    def one(axis_at, blocks):
        steps = jax.random.uniform(jax.random.fold_in(jax.random.fold_in(rng, 6), axis_at), (blocks,), jnp.float32, smallest / len(cuts), high / len(cuts))
        return jnp.repeat(jnp.exp(steps), shape[axis_at] // blocks).reshape((-1,) + (1,) * (len(shape) - axis_at - 1))

    gain = one(*cuts[0])
    for cut in cuts[1:]:
        gain = gain * one(*cut)
    return gain


def setup_inputs(seed: int = 0) -> dict:
    seeds = jax.random.split(jax.random.key(seed), 6)
    density = draw_density(jax.random.fold_in(seeds[5], 71), 0)
    flux_x = draw_flux_x(jax.random.fold_in(seeds[5], 71), 0)
    flux_y = draw_flux_y(jax.random.fold_in(seeds[5], 71), 0)
    congestion = jnp.clip(jnp.exp(math.log(5.0) - 3.218876 * jax.random.uniform(seeds[3], (NT, NX, NY), jnp.float32) ** block_scale(seeds[3], (NT, NX, NY), ((0, 8), (1, 8), (2, 8)), -0.2, 0.2)), 0.2, 5.0)
    initial_density = jnp.clip(0.25 + 2.25 * jax.random.uniform(seeds[4], (NX, NY), jnp.float32) ** block_scale(seeds[4], (NX, NY), ((0, 8), (1, 8)), -0.2, 0.2), 0.25, 2.5)
    return {"density": density, "flux_x": flux_x, "flux_y": flux_y, "congestion": congestion, "initial_density": initial_density}


step_gamma = 1.0


def proximal(density, flux_x, flux_y, congestion):
    speed_sq = flux_x * flux_x + flux_y * flux_y
    slope_coef = 1.0 + step_gamma * congestion
    mass_new = jnp.zeros_like(density)
    for newton in range(NEWTON):
        shifted = mass_new + step_gamma
        mismatch = slope_coef * mass_new - density - step_gamma * speed_sq / (2.0 * shifted * shifted)
        derivative = slope_coef + step_gamma * speed_sq / (shifted * shifted * shifted)
        mass_new = mass_new - mismatch / derivative
    shrink = mass_new / (mass_new + step_gamma)
    return mass_new, flux_x * shrink, flux_y * shrink


def laplacian(potential):
    earlier = jnp.concatenate([potential[:1], potential[:-1]], 0)
    later = jnp.concatenate([potential[1:], jnp.zeros_like(potential[:1])], 0)
    result = 6.0 * potential - earlier - later
    result = result - jnp.roll(potential, 1, 1) - jnp.roll(potential, -1, 1)
    return result - jnp.roll(potential, 1, 2) - jnp.roll(potential, -1, 2)


def reference(density, flux_x, flux_y, congestion, initial_density):
    mass_new, prox_x, prox_y = proximal(density, flux_x, flux_y, congestion)
    earlier = jnp.concatenate([initial_density[None], mass_new[:-1]], 0)
    source = mass_new - earlier + prox_x - jnp.roll(prox_x, 1, 1) + prox_y - jnp.roll(prox_y, 1, 2)
    potential = jnp.zeros_like(source)
    residual = source
    direction = source
    norm_now = jnp.sum(residual * residual)
    for iteration in range(ITERS):
        applied = laplacian(direction)
        step_size = norm_now / jnp.sum(direction * applied)
        potential = potential + step_size * direction
        residual = residual - step_size * applied
        norm_next = jnp.sum(residual * residual)
        direction = residual + (norm_next / norm_now) * direction
        norm_now = norm_next
    later = jnp.concatenate([potential[1:], jnp.zeros_like(potential[:1])], 0)
    mass_out = mass_new - (potential - later)
    flux_x_out = prox_x - (potential - jnp.roll(potential, -1, 1))
    flux_y_out = prox_y - (potential - jnp.roll(potential, -1, 2))
    return (mass_out, flux_x_out, flux_y_out)
```

```python
import functools
import itertools

import jax
import jax.numpy as jnp
from jax import lax
from jax.experimental import pallas as pl
from jax.experimental.pallas import tpu as pltpu
from jax.sharding import PartitionSpec as P

MESH = pl.DeviceIdType.MESH
NEWTON = 6
F32 = jnp.float32
TP, XR, TILES = 13, 72, 9


def roll(v, shift, axis):
    return pltpu.roll(v, shift, axis)


def group_a(c):
    peers = []
    for dz, dc in itertools.product(range(8), range(2)):
        if dz or dc:
            ta = c["ta"] + dc * (1 - 2 * lax.rem(c["ta"], 2))
            peers.append((min(dz, 8 - dz), (ta, c["gx"], lax.rem(c["gy"] + dz, 8))))
    return [p for _, p in sorted(peers, key=lambda e: -e[0])]


def group_b(c):
    y, x = (c["gx"] // 4) * 4 + c["ta"] // 2, lax.rem(c["gx"], 4)
    peers = []
    for dy, dx in itertools.product(range(8), range(4)):
        if dy or dx:
            yy, xx = lax.rem(y + dy, 8), lax.rem(x + dx, 4)
            at = (lax.rem(yy, 4) * 2 + lax.rem(c["ta"], 2), (yy // 4) * 4 + xx, c["gy"])
            peers.append((min(dy, 8 - dy) + min(dx, 4 - dx), at))
    return [p for _, p in sorted(peers, key=lambda e: -e[0])]


def kernel(
    d_hbm, fx_hbm, fy_hbm, c_hbm, i_hbm,
    mo_ref, xo_ref, yo_ref,
    d_ref, fx_ref, fy_ref, c_ref, i_ref, mass, px, py,
    eb, e1, e2, px0, pxm, m0, mm, pyq,
    s_xp, s_xm, s_pp, s_pm, s_mp, s_mm, s_p0, s_m0,
    r_xm, r_xp, r_mm, r_mp, r_pm, r_pp, r_m0, r_p0,
    s_yp, s_ym, r_ym, r_yp, buf_a, buf_b,
    in_sem, ss, rs, ra_send, ra_recv, rb_send, rb_recv,
):
    c = {a: lax.axis_index(a) for a in ("ta", "gx", "gy")}
    ta = c["ta"]
    has_m, has_p = ta > 0, ta < 7
    gxp, gxm = lax.rem(c["gx"] + 1, 8), lax.rem(c["gx"] + 7, 8)
    gyp, gym = lax.rem(c["gy"] + 1, 8), lax.rem(c["gy"] + 7, 8)
    peers_a, peers_b = group_a(c), group_b(c)

    def at(dt, gx):
        return (ta + dt, gx, c["gy"])

    bar = pltpu.get_barrier_semaphore()

    def greet(peer):
        pl.semaphore_signal(bar, inc=1, device_id=peer, device_id_type=MESH)

    for peer in peers_b:
        greet(peer)

    odd = lax.rem(ta, 2) == 1
    away_p = jnp.logical_and(has_p, odd)
    away_m = jnp.logical_and(has_m, jnp.logical_not(odd))

    @pl.when(has_p)
    def _():
        greet(at(1, gxp))
        greet(at(1, gxm))

    @pl.when(has_m)
    def _():
        greet(at(-1, gxp))
        greet(at(-1, gxm))

    @pl.when(away_p)
    def _():
        greet(at(1, c["gx"]))

    @pl.when(away_m)
    def _():
        greet(at(-1, c["gx"]))

    for peer in peers_a:
        greet(peer)

    loads = [
        pltpu.make_async_copy(a, b, in_sem.at[i])
        for i, (a, b) in enumerate(
            ((d_hbm, d_ref), (fx_hbm, fx_ref), (fy_hbm, fy_ref), (c_hbm, c_ref), (i_hbm, i_ref))
        )
    ]
    for copy in loads:
        copy.start()
    for copy in loads:
        copy.wait()

    lane64 = lax.broadcasted_iota(jnp.int32, (64, 128), 1)
    row64 = lax.broadcasted_iota(jnp.int32, (64, 128), 0)
    lane8 = lax.broadcasted_iota(jnp.int32, (8, 128), 1)
    sub8 = lax.broadcasted_iota(jnp.int32, (8, 128), 0)

    def newton(t, carry):
        before, packed = carry
        d, fx, fy = d_ref[t], fx_ref[t], fy_ref[t]
        q = fx * fx + fy * fy
        a = 1.0 + c_ref[t]
        m = (d + 0.5 * q) / (a + q)
        for _ in range(NEWTON - 1):
            s = m + 1.0
            s3 = s * s * s
            m = (d * s3 + q * (1.5 * s - 1.0)) / (a * s3 + q)
        shrink = m / (m + 1.0)
        vx, vy = fx * shrink, fy * shrink
        mass[t] = m
        px[t] = vx
        py[t] = vy
        b = m - before
        b = b + vx - jnp.where(row64 == 0, 0.0, roll(vx, 1, 0))
        b = b + vy - jnp.where(lane64 == 0, 0.0, roll(vy, 1, 1))
        eb[t + 2, 0:64, :] = b
        px0[pl.ds(t + 2, 1), :] = vx[63:64]
        for tile in range(8):
            k = t * TILES + tile
            packed = jnp.where(
                lane8 == k, roll(vy[8 * tile : 8 * tile + 8], k + 1, 1), packed
            )
        return m, packed

    start = jnp.where(ta == 0, i_ref[...], 0.0)
    m7, py127 = lax.fori_loop(0, 8, newton, (start, jnp.zeros((8, 128), F32)))

    for t in range(8):
        s_xp[2 * t : 2 * t + 2, :] = eb[t + 2, 62:64, :]
        s_xm[3 * t : 3 * t + 3, :] = eb[t + 2, 0:3, :]
    s_xp[16:24, :] = px0[2:10, :]
    s_xp[24:26, :] = m7[62:64]
    s_xp[26:28, :] = py127[6:8]
    s_xm[24:27, :] = m7[0:3]
    s_xm[27:30, :] = py127[0:3]
    for j in range(2):
        s_pp[2 * j : 2 * j + 2, :] = eb[8 + j, 62:64, :]
        s_pm[3 * j : 3 * j + 3, :] = eb[8 + j, 0:3, :]
    s_pp[4:6, :] = px0[8:10, :]
    s_pp[6:8, :] = m7[62:64]
    s_pp[8:10, :] = py127[6:8]
    s_pm[6:9, :] = m7[0:3]
    s_pm[9:12, :] = py127[0:3]
    for j in range(3):
        s_mp[2 * j : 2 * j + 2, :] = eb[2 + j, 62:64, :]
        s_mm[3 * j : 3 * j + 3, :] = eb[2 + j, 0:3, :]
    s_mp[6:9, :] = px0[2:5, :]
    s_mp[9:11, :] = py127[6:8]
    s_mm[9:12, :] = py127[0:3]
    s_p0[0:8, :] = py127
    s_p0[8:10, :] = px0[8:10, :]
    s_m0[0:8, :] = py127
    s_m0[8:11, :] = px0[2:5, :]

    def one(flag):
        return jnp.where(flag, 1, 0)

    greeted = len(peers_a) + len(peers_b) + 2 * one(has_p) + 2 * one(has_m)
    pl.semaphore_wait(bar, greeted + one(away_p) + one(away_m))

    def remote(i, src, dst, peer):
        return pltpu.make_async_remote_copy(
            src_ref=src, dst_ref=dst, send_sem=ss.at[i], recv_sem=rs.at[i],
            device_id=peer, device_id_type=MESH,
        )

    x_p = remote(0, s_xp, r_xm, at(0, gxp))
    x_m = remote(1, s_xm, r_xp, at(0, gxm))
    t_p = [
        remote(2, s_pp, r_mm, at(1, gxp)),
        remote(3, s_pm, r_mp, at(1, gxm)),
        remote(4, s_p0, r_m0, at(1, c["gx"])),
        remote(5, eb.at[8:10, 0:64], eb.at[0:2, 0:64], at(1, c["gx"])),
        remote(6, mass.at[7], mm.at[0:64], at(1, c["gx"])),
    ]
    t_m = [
        remote(7, s_mp, r_pm, at(-1, gxp)),
        remote(8, s_mm, r_pp, at(-1, gxm)),
        remote(9, s_m0, r_p0, at(-1, c["gx"])),
        remote(10, eb.at[2:5, 0:64], eb.at[10:13, 0:64], at(-1, c["gx"])),
    ]

    @pl.when(has_p)
    def _():
        for copy in t_p[:2]:
            copy.start()

    @pl.when(has_m)
    def _():
        for copy in t_m[:2]:
            copy.start()

    x_p.start()
    x_m.start()

    @pl.when(has_m)
    def _():
        for copy in t_m[2:]:
            copy.start()

    @pl.when(has_p)
    def _():
        for copy in t_p[2:]:
            copy.start()

    m0[0:64, :] = m7

    x_p.wait()
    x_m.wait()

    @pl.when(has_p)
    def _():
        for copy in t_p:
            copy.wait_send()

    @pl.when(has_m)
    def _():
        for copy in t_m:
            copy.wait_send()

    for t in range(8):
        eb[t + 2, 64:67, :] = r_xp[3 * t : 3 * t + 3, :]
        eb[t + 2, 70:72, :] = r_xm[2 * t : 2 * t + 2, :]
    pxm[2:10, :] = r_xm[16:24, :]
    m0[64:67, :] = r_xp[24:27, :]
    m0[70:72, :] = r_xm[24:26, :]
    pyq[0, 0:3, :] = r_xp[27:30, :]
    pyq[0, 6:8, :] = r_xm[26:28, :]

    @pl.when(has_m)
    def _():
        for copy in t_p:
            copy.wait_recv()
        for j in range(2):
            eb[j, 64:67, :] = r_mp[3 * j : 3 * j + 3, :]
            eb[j, 70:72, :] = r_mm[2 * j : 2 * j + 2, :]
        pxm[0:2, :] = r_mm[4:6, :]
        px0[0:2, :] = r_m0[8:10, :]
        mm[64:67, :] = r_mp[6:9, :]
        mm[70:72, :] = r_mm[6:8, :]
        pyq[1, 0:3, :] = r_mp[9:12, :]
        pyq[1, 6:8, :] = r_mm[8:10, :]
        eb[2] = eb[2] - mm[...]

    @pl.when(has_p)
    def _():
        for copy in t_m:
            copy.wait_recv()
        for j in range(3):
            eb[10 + j, 64:67, :] = r_pp[3 * j : 3 * j + 3, :]
            eb[10 + j, 70:72, :] = r_pm[2 * j : 2 * j + 2, :]
        pxm[10:13, :] = r_pm[6:9, :]
        px0[10:13, :] = r_p0[8:11, :]
        pyq[2, 0:3, :] = r_pp[9:12, :]
        pyq[2, 6:8, :] = r_pm[9:11, :]
        eb[10] = eb[10] - m0[...]

    for p in range(TP):
        eb[p, 0:1, :] = eb[p, 0:1, :] - pxm[p : p + 1, :]
        eb[p, 64:65, :] = eb[p, 64:65, :] - px0[p : p + 1, :]

    tile_of, plane_of = lax.rem(lane8, TILES), lane8 // TILES

    def side(i, low, high):
        v = pyq[i]
        return jnp.where(sub8 < 4, roll(v, low, 1), roll(v, high, 1))

    pyo = jnp.where(tile_of == 8, side(0, 26, 19), roll(py127, 18, 1))
    pyl = jnp.where(tile_of == 8, side(1, 82, 75), roll(r_m0[0:8, :], 74, 1))
    pyh = jnp.where(tile_of == 8, side(2, 98, 91), roll(r_p0[0:8, :], 90, 1))
    mirror_l = jnp.where(plane_of == 1, roll(pyo, 119, 1), roll(pyo, 101, 1))
    mirror_h = jnp.where(plane_of == 11, -roll(pyo, 18, 1), -roll(pyo, 36, 1))
    mirror_h = jnp.where(plane_of == 10, 0.0, mirror_h)
    pyl = jnp.where(has_m, pyl, mirror_l)
    pyh = jnp.where(has_p, pyh, mirror_h)
    py0 = jnp.where(plane_of < 2, pyl, jnp.where(plane_of < 10, pyo, pyh))

    @pl.when(jnp.logical_not(has_m))
    def _():
        eb[1] = eb[2]
        eb[0] = eb[3]

    @pl.when(jnp.logical_not(has_p))
    def _():
        eb[10] = jnp.zeros((XR, 128), F32)
        eb[11] = -eb[9]
        eb[12] = -eb[8]

    def pack(p, cols):
        v = eb[p]
        new = []
        for col, packed in zip((126, 127, 0, 1, 2), cols):
            for tile in range(TILES):
                k = p * TILES + tile
                r = roll(v[8 * tile : 8 * tile + 8], lax.rem(k + 128 - col, 128), 1)
                packed = jnp.where(lane8 == k, r, packed)
            new.append(packed)
        return tuple(new)

    zero8 = jnp.zeros((8, 128), F32)
    b126, b127, b0, b1, b2 = lax.fori_loop(0, TP, pack, (zero8,) * 5)
    s_yp[0:8, :] = b126
    s_yp[8:16, :] = b127
    s_yp[16:24, :] = py0
    s_ym[0:8, :] = b0
    s_ym[8:16, :] = b1
    s_ym[16:24, :] = b2
    y_p = remote(11, s_yp, r_ym, (ta, c["gx"], gyp))
    y_m = remote(12, s_ym, r_yp, (ta, c["gx"], gym))
    y_p.start()
    y_m.start()
    y_p.wait()
    y_m.wait()
    bm2, bm1, pym = r_ym[0:8, :], r_ym[8:16, :], r_ym[16:24, :]
    b128, b129, b130 = r_yp[0:8, :] - py0, r_yp[8:16, :], r_yp[16:24, :]
    b0 = b0 - pym

    def around(v):
        up = roll(v, 7, 0)
        nxt = jnp.where(tile_of == 8, roll(up, 8, 1), roll(up, 127, 1))
        up = jnp.where(sub8 == 7, nxt, up)
        down = roll(v, 1, 0)
        prv = jnp.where(tile_of == 0, roll(down, 120, 1), roll(down, 1, 1))
        down = jnp.where(sub8 == 0, prv, down)
        return (roll(v, 9, 1) + roll(v, 119, 1)) + (down + up)

    um1 = around(bm1) + (bm2 + b0)
    u127 = around(b127) + (b126 + b128)
    u128 = around(b128) + (b127 + b129)
    u129 = around(b129) + (b128 + b130)
    w128 = around(u128) + (u127 + u129)

    lane72 = lax.broadcasted_iota(jnp.int32, (XR, 128), 1)

    def unpack(packed, p, lane, tiles):
        return jnp.concatenate(
            [roll(packed, lax.rem(128 + lane - p * TILES - t, 128), 1) for t in range(tiles)], 0
        )

    def fix(p, _):
        eb[p] = jnp.where(lane72 == 0, unpack(b0, p, 0, TILES), eb[p])
        return 0

    lax.fori_loop(0, TP, fix, 0)

    def spread(src, dst, left, right):
        def step(p, _):
            v = src[p]
            lo = jnp.where(lane72 == 0, unpack(left, p, 0, TILES), roll(v, 1, 1))
            hi = jnp.where(lane72 == 127, unpack(right, p, 127, TILES), roll(v, 127, 1))
            dst[p] = (src[p - 1] + src[p + 1]) + (roll(v, 1, 0) + roll(v, XR - 1, 0)) + (lo + hi)
            return 0

        return step

    lax.fori_loop(1, 12, spread(eb, e1, bm1, b128), 0)
    lax.fori_loop(2, 11, spread(e1, e2, um1, u128), 0)

    def fold(v):
        return jnp.sum(v.reshape(8, 8, 128), axis=0)

    def moments(p, acc):
        b, u, full = eb[p, 0:64, :], e1[p, 0:64, :], e2[p]
        w = full[0:64]
        hi = jnp.where(lane64 == 127, unpack(w128, p, 127, 8), roll(w, 127, 1))
        later = (e2[p + 1, 0:64, :] + roll(full, XR - 1, 0)[0:64]) + hi
        terms = (b * b, b * u, u * u, u * w, w * w, w * later)
        return tuple(a + fold(v) for a, v in zip(acc, terms))

    acc = lax.fori_loop(2, 10, moments, (zero8,) * 6)
    w0 = e2[2, 0:64, :]
    first = jnp.where(ta == 0, fold(w0 * w0), 0.0)
    acc = acc[:5] + (2.0 * acc[5] + first,)
    lane1 = lax.broadcasted_iota(jnp.int32, (1, 128), 1)
    row = jnp.zeros((1, 128), F32)
    for i, v in enumerate(acc):
        row = jnp.where(lane1 == i, jnp.sum(v, keepdims=True), row)

    def all_sum(buf, row, peers, send, recv):
        n = len(peers)
        buf[0] = row
        for i, peer in enumerate(peers):
            pltpu.make_async_remote_copy(
                src_ref=buf.at[0], dst_ref=buf.at[i + 1], send_sem=send, recv_sem=recv,
                device_id=peer, device_id_type=MESH,
            ).start()
        rest = pltpu.make_async_remote_copy(
            src_ref=buf.at[1 : n + 1], dst_ref=buf.at[1 : n + 1], send_sem=send, recv_sem=recv,
            device_id=peers[0], device_id_type=MESH,
        )
        rest.wait_recv()
        total = buf[0]
        for i in range(n):
            total = total + buf[i + 1]
        return total, rest

    row, sent_a = all_sum(buf_a, row, peers_a, ra_send, ra_recv)
    row, sent_b = all_sum(buf_b, row, peers_b, rb_send, rb_recv)
    n = [jnp.sum(jnp.where(lane1 == i, row, 0.0), axis=1, keepdims=True) for i in range(6)]

    g0, g1, g2, g3, g4 = (6.0 * n[i] - n[i + 1] for i in range(5))
    l1, l2 = g1 / g0, g2 / g0
    d1 = g2 - l1 * g1
    f1 = g3 - l2 * g1
    l3 = f1 / d1
    d2 = g4 - l2 * g2 - l3 * f1
    y1 = n[1] - l1 * n[0]
    y2 = n[2] - l2 * n[0] - l3 * y1
    c2 = y2 / d2
    c1 = y1 / d1 - l3 * c2
    c0 = n[0] / g0 - l1 * c1 - l2 * c2
    c0, c1, c2 = (jnp.broadcast_to(v, (8, 128)) for v in (c0, c1, c2))
    k0, k1, k2 = (jnp.broadcast_to(v[0:1], (XR, 128)) for v in (c0, c1, c2))

    v128 = c0 * b128 + c1 * u128 + c2 * w128

    def plane(p):
        return k0 * eb[p] + k1 * e1[p] + k2 * e2[p]

    def finish(t, v):
        p = t + 2
        nxt = plane(p + 1)
        v64 = v[0:64]
        hi = jnp.where(lane64 == 127, unpack(v128, p, 127, 8), roll(v64, 127, 1))
        mo_ref[t] = mass[t] - (v64 - nxt[0:64])
        xo_ref[t] = px[t] - (v64 - roll(v, XR - 1, 0)[0:64])
        yo_ref[t] = py[t] - (v64 - hi)
        return nxt

    lax.fori_loop(0, 8, finish, plane(2))
    sent_a.wait_send()
    sent_b.wait_send()


def body(density, flux_x, flux_y, congestion, initial_density):
    block = jax.ShapeDtypeStruct((8, 64, 128), F32)
    vm = lambda *s: pltpu.VMEM(s, F32)
    dma = pltpu.SemaphoreType.DMA
    return pl.pallas_call(
        kernel,
        out_shape=(block,) * 3,
        in_specs=[pl.BlockSpec(memory_space=pl.ANY)] * 5,
        out_specs=[pl.BlockSpec(memory_space=pltpu.VMEM)] * 3,
        scratch_shapes=[vm(8, 64, 128)] * 4
        + [vm(64, 128)]
        + [vm(8, 64, 128)] * 3
        + [vm(TP, XR, 128)] * 3
        + [vm(16, 128)] * 2
        + [vm(XR, 128)] * 2
        + [vm(3, 8, 128)]
        + [vm(32, 128)] * 2
        + [vm(16, 128)] * 6
        + [vm(32, 128)] * 2
        + [vm(16, 128)] * 6
        + [vm(24, 128)] * 4
        + [vm(16, 1, 128), vm(32, 1, 128)]
        + [dma((5,)), dma((13,)), dma((13,))]
        + [dma] * 4,
        compiler_params=pltpu.CompilerParams(collective_id=0, has_side_effects=True),
        name="prox_project",
    )(density, flux_x, flux_y, congestion, initial_density)


def solution(mesh):
    spec = P("ta", "gx", "gy")
    return jax.shard_map(
        body,
        mesh=mesh,
        in_specs=(spec,) * 4 + (P("gx", "gy"),),
        out_specs=(spec,) * 3,
        check_vma=False,
    )
```

```python
import functools
import itertools

import jax
import jax.numpy as jnp
from jax import lax
from jax.experimental import pallas as pl
from jax.experimental.pallas import tpu as pltpu
from jax.sharding import PartitionSpec as P

MESH = pl.DeviceIdType.MESH
NEWTON = 6
F32 = jnp.float32
TP, XR = 13, 72
VMEM_MAIN, VMEM_STORE = 16 * 2**20, 2**20


def roll(v, shift, axis):
    return pltpu.roll(v, shift, axis)


def group_a(c):
    peers = []
    for dz, dc in itertools.product(range(8), range(2)):
        if dz or dc:
            ta = c["ta"] + dc * (1 - 2 * lax.rem(c["ta"], 2))
            peers.append((min(dz, 8 - dz), (ta, c["gx"], lax.rem(c["gy"] + dz, 8))))
    return [p for _, p in sorted(peers, key=lambda e: -e[0])]


def group_b(c):
    y, x = (c["gx"] // 4) * 4 + c["ta"] // 2, lax.rem(c["gx"], 4)
    peers = []
    for dy, dx in itertools.product(range(8), range(4)):
        if dy or dx:
            yy, xx = lax.rem(y + dy, 8), lax.rem(x + dx, 4)
            at = (lax.rem(yy, 4) * 2 + lax.rem(c["ta"], 2), (yy // 4) * 4 + xx, c["gy"])
            peers.append((min(dy, 8 - dy) + min(dx, 4 - dx), at))
    return [p for _, p in sorted(peers, key=lambda e: -e[0])]


def kernel(
    d_hbm, fx_hbm, fy_hbm, c_hbm, i_hbm,
    mo_ref, xo_ref, yo_ref,
    d_ref, fx_ref, fy_ref, c_ref, i_ref, mass, px, py,
    eb, e1, e2, px0, pxm, m0, mm, pyo, pyl, pyh, diffs,
    s_xp, s_xm, s_pp, s_pm, s_mp, s_mm,
    r_xm, r_xp, r_mm, r_mp, r_pm, r_pp,
    s_yp, s_ym, r_ym, r_yp, buf_a, buf_b,
    in_sem, ss, rs, ra_send, ra_recv, rb_send, rb_recv,
):
    c = {a: lax.axis_index(a) for a in ("ta", "gx", "gy")}
    ta = c["ta"]
    has_m, has_p = ta > 0, ta < 7
    gxp, gxm = lax.rem(c["gx"] + 1, 8), lax.rem(c["gx"] + 7, 8)
    gyp, gym = lax.rem(c["gy"] + 1, 8), lax.rem(c["gy"] + 7, 8)
    peers_a, peers_b = group_a(c), group_b(c)

    def at(dt, gx):
        return (ta + dt, gx, c["gy"])

    bar = pltpu.get_barrier_semaphore()

    def greet(peer):
        pl.semaphore_signal(bar, inc=1, device_id=peer, device_id_type=MESH)

    for peer in peers_b:
        greet(peer)

    odd = lax.rem(ta, 2) == 1
    away_p = jnp.logical_and(has_p, odd)
    away_m = jnp.logical_and(has_m, jnp.logical_not(odd))

    @pl.when(has_p)
    def _():
        greet(at(1, gxp))
        greet(at(1, gxm))

    @pl.when(has_m)
    def _():
        greet(at(-1, gxp))
        greet(at(-1, gxm))

    @pl.when(away_p)
    def _():
        greet(at(1, c["gx"]))

    @pl.when(away_m)
    def _():
        greet(at(-1, c["gx"]))

    for peer in peers_a:
        greet(peer)

    loads = [
        pltpu.make_async_copy(a, b, in_sem.at[i])
        for i, (a, b) in enumerate(
            ((d_hbm, d_ref), (fx_hbm, fx_ref), (fy_hbm, fy_ref), (c_hbm, c_ref), (i_hbm, i_ref))
        )
    ]
    for copy in loads:
        copy.start()
    for copy in loads:
        copy.wait()

    lane64 = lax.broadcasted_iota(jnp.int32, (64, 128), 1)
    row64 = lax.broadcasted_iota(jnp.int32, (64, 128), 0)
    lane8 = lax.broadcasted_iota(jnp.int32, (8, 128), 1)
    lane72 = lax.broadcasted_iota(jnp.int32, (XR, 128), 1)
    slot8, plane8 = lax.rem(lane8, 8), lane8 // 8
    slot72 = lax.rem(lane72, 8)
    pyo[...] = jnp.zeros((XR, 128), F32)

    def newton(t, before):
        d, fx, fy = d_ref[t], fx_ref[t], fy_ref[t]
        q = fx * fx + fy * fy
        a = 1.0 + c_ref[t]
        m = (d + 0.5 * q) / (a + q)
        for _ in range(NEWTON - 1):
            s = m + 1.0
            s3 = s * s * s
            m = (d * s3 + q * (1.5 * s - 1.0)) / (a * s3 + q)
        shrink = m / (m + 1.0)
        vx, vy = fx * shrink, fy * shrink
        mass[t] = m
        px[t] = vx
        py[t] = vy
        b = m - before
        b = b + vx - jnp.where(row64 == 0, 0.0, roll(vx, 1, 0))
        b = b + vy - jnp.where(lane64 == 0, 0.0, roll(vy, 1, 1))
        eb[t + 2, 0:64, :] = b
        px0[pl.ds(t + 2, 1), :] = vx[63:64]
        pyo[0:64, :] = jnp.where(lane64 == 8 * t + 21, roll(vy, 8 * t + 22, 1), pyo[0:64, :])
        return m

    start = jnp.where(ta == 0, i_ref[...], 0.0)
    m7 = lax.fori_loop(0, 8, newton, start)

    for t in range(8):
        s_xp[2 * t : 2 * t + 2, :] = eb[t + 2, 62:64, :]
        s_xm[3 * t : 3 * t + 3, :] = eb[t + 2, 0:3, :]
    s_xp[16:24, :] = px0[2:10, :]
    s_xp[24:26, :] = m7[62:64]
    s_xp[26:28, :] = pyo[62:64, :]
    s_xm[24:27, :] = m7[0:3]
    s_xm[27:30, :] = pyo[0:3, :]
    for j in range(2):
        s_pp[2 * j : 2 * j + 2, :] = eb[8 + j, 62:64, :]
        s_pm[3 * j : 3 * j + 3, :] = eb[8 + j, 0:3, :]
    s_pp[4:6, :] = px0[8:10, :]
    s_pp[6:8, :] = m7[62:64]
    s_pp[8:10, :] = pyo[62:64, :]
    s_pm[6:9, :] = m7[0:3]
    s_pm[9:12, :] = pyo[0:3, :]
    for j in range(3):
        s_mp[2 * j : 2 * j + 2, :] = eb[2 + j, 62:64, :]
        s_mm[3 * j : 3 * j + 3, :] = eb[2 + j, 0:3, :]
    s_mp[6:9, :] = px0[2:5, :]
    s_mp[9:11, :] = pyo[62:64, :]
    s_mm[9:12, :] = pyo[0:3, :]
    def one(flag):
        return jnp.where(flag, 1, 0)

    greeted = len(peers_a) + len(peers_b) + 2 * one(has_p) + 2 * one(has_m)
    pl.semaphore_wait(bar, greeted + one(away_p) + one(away_m))

    def remote(i, src, dst, peer):
        return pltpu.make_async_remote_copy(
            src_ref=src, dst_ref=dst, send_sem=ss.at[i], recv_sem=rs.at[i],
            device_id=peer, device_id_type=MESH,
        )

    x_p = remote(0, s_xp, r_xm, at(0, gxp))
    x_m = remote(1, s_xm, r_xp, at(0, gxm))
    t_p = [
        remote(2, s_pp, r_mm, at(1, gxp)),
        remote(3, s_pm, r_mp, at(1, gxm)),
        remote(4, px0.at[8:10], px0.at[0:2], at(1, c["gx"])),
        remote(5, eb.at[8:10, 0:64], eb.at[0:2, 0:64], at(1, c["gx"])),
        remote(6, mass.at[7], mm.at[0:64], at(1, c["gx"])),
        remote(7, pyo.at[0:64], pyl.at[0:64], at(1, c["gx"])),
    ]
    t_m = [
        remote(8, s_mp, r_pm, at(-1, gxp)),
        remote(9, s_mm, r_pp, at(-1, gxm)),
        remote(10, px0.at[2:5], px0.at[10:13], at(-1, c["gx"])),
        remote(11, eb.at[2:5, 0:64], eb.at[10:13, 0:64], at(-1, c["gx"])),
        remote(12, pyo.at[0:64], pyh.at[0:64], at(-1, c["gx"])),
    ]

    @pl.when(has_p)
    def _():
        for copy in t_p[:2]:
            copy.start()

    @pl.when(has_m)
    def _():
        for copy in t_m[:2]:
            copy.start()

    x_p.start()
    x_m.start()

    @pl.when(has_m)
    def _():
        for copy in t_m[2:]:
            copy.start()

    @pl.when(has_p)
    def _():
        for copy in t_p[2:]:
            copy.start()

    m0[0:64, :] = m7

    x_p.wait()
    x_m.wait()

    @pl.when(has_p)
    def _():
        for copy in t_p:
            copy.wait_send()

    @pl.when(has_m)
    def _():
        for copy in t_m:
            copy.wait_send()

    for t in range(8):
        eb[t + 2, 64:67, :] = r_xp[3 * t : 3 * t + 3, :]
        eb[t + 2, 70:72, :] = r_xm[2 * t : 2 * t + 2, :]
    pxm[2:10, :] = r_xm[16:24, :]
    m0[64:67, :] = r_xp[24:27, :]
    m0[70:72, :] = r_xm[24:26, :]
    pyo[64:67, :] = r_xp[27:30, :]
    pyo[70:72, :] = r_xm[26:28, :]

    @pl.when(has_m)
    def _():
        for copy in t_p:
            copy.wait_recv()
        for j in range(2):
            eb[j, 64:67, :] = r_mp[3 * j : 3 * j + 3, :]
            eb[j, 70:72, :] = r_mm[2 * j : 2 * j + 2, :]
        pxm[0:2, :] = r_mm[4:6, :]
        mm[64:67, :] = r_mp[6:9, :]
        mm[70:72, :] = r_mm[6:8, :]
        pyl[64:67, :] = r_mp[9:12, :]
        pyl[70:72, :] = r_mm[8:10, :]
        eb[2] = eb[2] - mm[...]

    @pl.when(has_p)
    def _():
        for copy in t_m:
            copy.wait_recv()
        for j in range(3):
            eb[10 + j, 64:67, :] = r_pp[3 * j : 3 * j + 3, :]
            eb[10 + j, 70:72, :] = r_pm[2 * j : 2 * j + 2, :]
        pxm[10:13, :] = r_pm[6:9, :]
        pyh[64:67, :] = r_pp[9:12, :]
        pyh[70:72, :] = r_pm[9:11, :]
        eb[10] = eb[10] - m0[...]

    for p in range(TP):
        eb[p, 0:1, :] = eb[p, 0:1, :] - pxm[p : p + 1, :]
        eb[p, 64:65, :] = eb[p, 64:65, :] - px0[p : p + 1, :]

    own = pyo[...]
    low = jnp.where(lane72 < 8, roll(own, 104, 1), roll(own, 120, 1))
    high = jnp.where(lane72 < 96, -roll(own, 16, 1), -roll(own, 32, 1))
    high = jnp.where(lane72 < 88, 0.0, high)
    low = jnp.where(has_m, roll(pyl[...], 64, 1), low)
    high = jnp.where(has_p, roll(pyh[...], 64, 1), high)
    py0 = jnp.where(lane72 < 16, low, jnp.where(lane72 < 80, own, high))

    @pl.when(jnp.logical_not(has_m))
    def _():
        eb[1] = eb[2]
        eb[0] = eb[3]

    @pl.when(jnp.logical_not(has_p))
    def _():
        eb[10] = jnp.zeros((XR, 128), F32)
        eb[11] = -eb[9]
        eb[12] = -eb[8]

    def pack(p, strips):
        v = eb[p]
        here = lane72 // 8 == p
        shifted = (roll(v, 8 * p + 2, 1), roll(v, 8 * p + 5, 1))
        return tuple(jnp.where(here, r, strip) for r, strip in zip(shifted, strips))

    zero8, zero72 = jnp.zeros((8, 128), F32), jnp.zeros((XR, 128), F32)
    left, right = lax.fori_loop(0, TP, pack, (zero72, zero72))
    s_yp[...] = jnp.where(slot72 == 5, py0, right)
    s_ym[...] = left
    y_p = remote(13, s_yp, r_ym, (ta, c["gx"], gyp))
    y_m = remote(14, s_ym, r_yp, (ta, c["gx"], gym))
    y_p.start()
    y_m.start()

    def spread(src, dst):
        def step(p, _):
            v = src[p]
            ends = roll(v, 1, 1) + roll(v, 127, 1)
            dst[p] = (src[p - 1] + src[p + 1]) + (roll(v, 1, 0) + roll(v, XR - 1, 0)) + ends
            return 0

        return step

    def fold(v):
        return jnp.sum(v.reshape(8, 8, 128), axis=0)

    def moments(p, acc):
        b, u, full = eb[p, 0:64, :], e1[p, 0:64, :], e2[p]
        w = full[0:64]
        later = e2[p + 1, 0:64, :] + roll(full, XR - 1, 0)[0:64]
        terms = (b * b, b * u, u * u, u * w, w * w, w * later, w * roll(w, 127, 1))
        return tuple(a + fold(v) for a, v in zip(acc, terms))

    lax.fori_loop(1, 12, spread(eb, e1), 0)
    lax.fori_loop(2, 11, spread(e1, e2), 0)
    acc = lax.fori_loop(2, 10, moments, (zero8,) * 7)
    w0 = e2[2, 0:64, :]
    first = fold(w0 * w0)

    y_p.wait()
    y_m.wait()
    near = roll(r_ym[...], 125, 1)
    left = jnp.where(slot72 < 2, near, left) - jnp.where(slot72 == 2, near, 0.0)
    near = roll(r_yp[...], 3, 1)
    right = jnp.where(slot72 >= 5, near, right) - jnp.where(slot72 == 5, py0, 0.0)

    def around(v):
        return (
            (roll(v, 8, 1) + roll(v, 120, 1))
            + (roll(v, 1, 0) + roll(v, XR - 1, 0))
            + (roll(v, 1, 1) + roll(v, 127, 1))
        )

    strips = []
    inner = jnp.logical_and(lane8 >= 3, lane8 < 126)
    acc = [jnp.where(inner, v, 0.0) for v in acc[:6]] + [jnp.where(lane8 == 125, 0.0, jnp.where(inner, acc[6], 0.0))]
    first = jnp.where(inner, first, 0.0)
    block = jnp.logical_and(plane8 >= 2, plane8 < 10)
    for v, lo, hi in ((left, 2, 5), (right, 3, 5)):
        u = around(v)
        w = around(u)
        strips.append((v, u, w))
        later = (roll(w, 120, 1) + roll(w, XR - 1, 0))[0:64]
        v, u, w = v[0:64], u[0:64], w[0:64]
        cells = jnp.logical_and(block, jnp.logical_and(slot8 >= lo, slot8 < hi))
        pairs = jnp.logical_and(block, jnp.logical_and(slot8 >= 2, slot8 < 5))
        ww = fold(w * w)
        terms = [fold(e) for e in (v * v, v * u, u * u, u * w)] + [ww, fold(w * later)]
        acc = [a + jnp.where(cells, e, 0.0) for a, e in zip(acc, terms)] + [
            acc[6] + jnp.where(pairs, fold(w * roll(w, 127, 1)), 0.0)
        ]
        first = first + jnp.where(jnp.logical_and(cells, plane8 == 2), ww, 0.0)
    first = jnp.where(ta == 0, first, 0.0)
    acc = acc[:5] + [2.0 * (acc[5] + acc[6]) + first]
    lane1 = lax.broadcasted_iota(jnp.int32, (1, 128), 1)
    row = jnp.zeros((1, 128), F32)
    for i, v in enumerate(acc):
        row = jnp.where(lane1 == i, jnp.sum(v, keepdims=True), row)

    def send_all(buf, row, peers, send, recv):
        n = len(peers)
        buf[0] = row
        for i, peer in enumerate(peers):
            pltpu.make_async_remote_copy(
                src_ref=buf.at[0], dst_ref=buf.at[i + 1], send_sem=send, recv_sem=recv,
                device_id=peer, device_id_type=MESH,
            ).start()
        return pltpu.make_async_remote_copy(
            src_ref=buf.at[1 : n + 1], dst_ref=buf.at[1 : n + 1], send_sem=send, recv_sem=recv,
            device_id=peers[0], device_id_type=MESH,
        )

    def sum_all(buf, n):
        total = buf[0]
        for i in range(n):
            total = total + buf[i + 1]
        return total

    sent_a = send_all(buf_a, row, peers_a, ra_send, ra_recv)

    def differences(i, e):
        sl, sr = strips[0][i], strips[1][i]

        def whole(p):
            v = jnp.where(lane72 < 3, roll(sl, 126 - 8 * p, 1), e[p])
            return jnp.where(lane72 >= 126, roll(sr, 123 - 8 * p, 1), v)

        def step(t, v):
            p = t + 2
            nxt = whole(p + 1)
            v64 = v[0:64]
            hi = roll(jnp.where(lane64 == 0, roll(sr[0:64], 123 - 8 * p, 1), v64), 127, 1)
            diffs[i, 0, t] = v64 - nxt[0:64]
            diffs[i, 1, t] = v64 - roll(v, XR - 1, 0)[0:64]
            diffs[i, 2, t] = v64 - hi
            return nxt

        lax.fori_loop(0, 8, step, whole(2))

    for i, e in enumerate((eb, e1, e2)):
        differences(i, e)

    sent_a.wait_recv()
    row = sum_all(buf_a, len(peers_a))
    sent_b = send_all(buf_b, row, peers_b, rb_send, rb_recv)
    sent_b.wait_recv()
    row = sum_all(buf_b, len(peers_b))
    n = [jnp.sum(jnp.where(lane1 == i, row, 0.0), axis=1, keepdims=True) for i in range(6)]

    g0, g1, g2, g3, g4 = (6.0 * n[i] - n[i + 1] for i in range(5))
    l1, l2 = g1 / g0, g2 / g0
    d1 = g2 - l1 * g1
    f1 = g3 - l2 * g1
    l3 = f1 / d1
    d2 = g4 - l2 * g2 - l3 * f1
    y1 = n[1] - l1 * n[0]
    y2 = n[2] - l2 * n[0] - l3 * y1
    c2 = y2 / d2
    c1 = y1 / d1 - l3 * c2
    c0 = n[0] / g0 - l1 * c1 - l2 * c2
    c0, c1, c2 = (jnp.broadcast_to(v, (64, 128)) for v in (c0, c1, c2))

    def finish(t, _):
        for k, (old, out) in enumerate(((mass, mo_ref), (px, xo_ref), (py, yo_ref))):
            step = c0 * diffs[0, k, t] + c1 * diffs[1, k, t] + c2 * diffs[2, k, t]
            out[t] = old[t] - step
        return 0

    lax.fori_loop(0, 8, finish, 0)
    sent_a.wait_send()
    sent_b.wait_send()


def store(a_ref, b_ref, c_ref, a_out, b_out, c_out, sem):
    pairs = ((a_ref, a_out), (b_ref, b_out), (c_ref, c_out))
    copies = [pltpu.make_async_copy(src, dst, sem.at[i]) for i, (src, dst) in enumerate(pairs)]
    for copy in copies:
        copy.start()
    for copy in copies:
        copy.wait()


def body(density, flux_x, flux_y, congestion, initial_density):
    block = jax.ShapeDtypeStruct((8, 64, 128), F32)
    vm = lambda *s: pltpu.VMEM(s, F32)
    dma = pltpu.SemaphoreType.DMA
    arrays = (density, flux_x, flux_y, congestion, initial_density)
    arrays = [pltpu.with_memory_space_constraint(a, pltpu.HBM) for a in arrays]
    outs = pl.pallas_call(
        kernel,
        out_shape=(block,) * 3,
        in_specs=[pl.BlockSpec(memory_space=pltpu.HBM)] * 5,
        out_specs=[pl.BlockSpec(memory_space=pltpu.VMEM)] * 3,
        scratch_shapes=[vm(8, 64, 128)] * 4
        + [vm(64, 128)]
        + [vm(8, 64, 128)] * 3
        + [vm(TP, XR, 128)] * 3
        + [vm(16, 128)] * 2
        + [vm(XR, 128)] * 5
        + [vm(3, 3, 8, 64, 128)]
        + [vm(32, 128)] * 2
        + [vm(16, 128)] * 4
        + [vm(32, 128)] * 2
        + [vm(16, 128)] * 4
        + [vm(XR, 128)] * 4
        + [vm(16, 1, 128), vm(32, 1, 128)]
        + [dma((5,)), dma((15,)), dma((15,))]
        + [dma] * 4,
        compiler_params=pltpu.CompilerParams(
            collective_id=0, has_side_effects=True, vmem_limit_bytes=VMEM_MAIN
        ),
        name="prox_project",
    )(*arrays)
    return pl.pallas_call(
        store,
        out_shape=(block,) * 3,
        in_specs=[pl.BlockSpec(memory_space=pltpu.VMEM)] * 3,
        out_specs=[pl.BlockSpec(memory_space=pltpu.HBM)] * 3,
        scratch_shapes=[dma((3,))],
        compiler_params=pltpu.CompilerParams(vmem_limit_bytes=VMEM_STORE),
        name="store",
    )(*outs)


def solution(mesh):
    spec = P("ta", "gx", "gy")
    return jax.shard_map(
        body,
        mesh=mesh,
        in_specs=(spec,) * 4 + (P("gx", "gy"),),
        out_specs=(spec,) * 3,
        check_vma=False,
    )
```

```python
import functools
import itertools

import jax
import jax.numpy as jnp
from jax import lax
from jax.experimental import pallas as pl
from jax.experimental.pallas import tpu as pltpu
from jax.sharding import PartitionSpec as P

MESH = pl.DeviceIdType.MESH
NEWTON = 6
F32 = jnp.float32
TP, XR = 13, 72
VMEM_MAIN, VMEM_STORE = 16 * 2**20, 2**20


def roll(v, shift, axis):
    return pltpu.roll(v, shift, axis)


def group_a(c):
    peers = []
    for dz, dc in itertools.product(range(8), range(2)):
        if dz or dc:
            ta = c["ta"] + dc * (1 - 2 * lax.rem(c["ta"], 2))
            peers.append((min(dz, 8 - dz), (ta, c["gx"], lax.rem(c["gy"] + dz, 8))))
    return [p for _, p in sorted(peers, key=lambda e: -e[0])]


def group_b(c):
    y, x = (c["gx"] // 4) * 4 + c["ta"] // 2, lax.rem(c["gx"], 4)
    peers = []
    for dy, dx in itertools.product(range(8), range(4)):
        if dy or dx:
            yy, xx = lax.rem(y + dy, 8), lax.rem(x + dx, 4)
            at = (lax.rem(yy, 4) * 2 + lax.rem(c["ta"], 2), (yy // 4) * 4 + xx, c["gy"])
            peers.append((min(dy, 8 - dy) + min(dx, 4 - dx), at))
    return [p for _, p in sorted(peers, key=lambda e: -e[0])]


def kernel(
    d_hbm, fx_hbm, fy_hbm, c_hbm, i_hbm,
    mo_ref, xo_ref, yo_ref,
    d_ref, fx_ref, fy_ref, c_ref, i_ref, mass, px, py,
    eb, e1, e2, px0, pxm, m0, mm, pyo, pyl, pyh, diffs,
    s_xp, s_xm, s_pp, s_pm, s_mp, s_mm,
    r_xm, r_xp, r_mm, r_mp, r_pm, r_pp,
    s_yp, s_ym, r_ym, r_yp, buf_a, buf_b,
    in_sem, ss, rs, ra_send, ra_recv, rb_send, rb_recv,
):
    c = {a: lax.axis_index(a) for a in ("ta", "gx", "gy")}
    ta = c["ta"]
    has_m, has_p = ta > 0, ta < 7
    gxp, gxm = lax.rem(c["gx"] + 1, 8), lax.rem(c["gx"] + 7, 8)
    gyp, gym = lax.rem(c["gy"] + 1, 8), lax.rem(c["gy"] + 7, 8)
    peers_a, peers_b = group_a(c), group_b(c)

    def at(dt, gx):
        return (ta + dt, gx, c["gy"])

    loads = [
        pltpu.make_async_copy(a, b, in_sem.at[i])
        for i, (a, b) in enumerate(
            ((d_hbm, d_ref), (fx_hbm, fx_ref), (fy_hbm, fy_ref), (c_hbm, c_ref), (i_hbm, i_ref))
        )
    ]
    for copy in loads:
        copy.start()

    bar = pltpu.get_barrier_semaphore()

    def greet(peer):
        pl.semaphore_signal(bar, inc=1, device_id=peer, device_id_type=MESH)

    odd = lax.rem(ta, 2) == 1
    away_p = jnp.logical_and(has_p, odd)
    away_m = jnp.logical_and(has_m, jnp.logical_not(odd))

    @pl.when(has_p)
    def _():
        greet(at(1, gxp))
        greet(at(1, gxm))

    @pl.when(has_m)
    def _():
        greet(at(-1, gxp))
        greet(at(-1, gxm))

    for peer in peers_b:
        greet(peer)

    @pl.when(away_p)
    def _():
        greet(at(1, c["gx"]))

    @pl.when(away_m)
    def _():
        greet(at(-1, c["gx"]))

    for peer in peers_a:
        greet(peer)

    for copy in loads:
        copy.wait()

    lane64 = lax.broadcasted_iota(jnp.int32, (64, 128), 1)
    row64 = lax.broadcasted_iota(jnp.int32, (64, 128), 0)
    lane8 = lax.broadcasted_iota(jnp.int32, (8, 128), 1)
    lane72 = lax.broadcasted_iota(jnp.int32, (XR, 128), 1)
    slot8, plane8 = lax.rem(lane8, 8), lane8 // 8
    slot72 = lax.rem(lane72, 8)
    pyo[...] = jnp.zeros((XR, 128), F32)

    def newton(t, before):
        d, fx, fy = d_ref[t], fx_ref[t], fy_ref[t]
        q = fx * fx + fy * fy
        a = 1.0 + c_ref[t]
        m = (d + 0.5 * q) / (a + q)
        for _ in range(NEWTON - 1):
            s = m + 1.0
            s3 = s * s * s
            m = (d * s3 + q * (1.5 * s - 1.0)) / (a * s3 + q)
        shrink = m / (m + 1.0)
        vx, vy = fx * shrink, fy * shrink
        mass[t] = m
        px[t] = vx
        py[t] = vy
        b = m - before
        b = b + vx - jnp.where(row64 == 0, 0.0, roll(vx, 1, 0))
        b = b + vy - jnp.where(lane64 == 0, 0.0, roll(vy, 1, 1))
        eb[t + 2, 0:64, :] = b
        px0[pl.ds(t + 2, 1), :] = vx[63:64]
        pyo[0:64, :] = jnp.where(lane64 == 8 * t + 21, roll(vy, 8 * t + 22, 1), pyo[0:64, :])
        return m

    start = jnp.where(ta == 0, i_ref[...], 0.0)
    m7 = lax.fori_loop(0, 8, newton, start)

    for t in range(8):
        s_xp[2 * t : 2 * t + 2, :] = eb[t + 2, 62:64, :]
        s_xm[3 * t : 3 * t + 3, :] = eb[t + 2, 0:3, :]
    s_xp[16:24, :] = px0[2:10, :]
    s_xp[24:26, :] = m7[62:64]
    s_xp[26:28, :] = pyo[62:64, :]
    s_xm[24:27, :] = m7[0:3]
    s_xm[27:30, :] = pyo[0:3, :]
    for j in range(2):
        s_pp[2 * j : 2 * j + 2, :] = eb[8 + j, 62:64, :]
        s_pm[3 * j : 3 * j + 3, :] = eb[8 + j, 0:3, :]
    s_pp[4:6, :] = px0[8:10, :]
    s_pp[6:8, :] = m7[62:64]
    s_pp[8:10, :] = pyo[62:64, :]
    s_pm[6:9, :] = m7[0:3]
    s_pm[9:12, :] = pyo[0:3, :]
    for j in range(3):
        s_mp[2 * j : 2 * j + 2, :] = eb[2 + j, 62:64, :]
        s_mm[3 * j : 3 * j + 3, :] = eb[2 + j, 0:3, :]
    s_mp[6:9, :] = px0[2:5, :]
    s_mp[9:11, :] = pyo[62:64, :]
    s_mm[9:12, :] = pyo[0:3, :]
    def one(flag):
        return jnp.where(flag, 1, 0)

    greeted = len(peers_a) + len(peers_b) + 2 * one(has_p) + 2 * one(has_m)
    pl.semaphore_wait(bar, greeted + one(away_p) + one(away_m))

    def remote(i, src, dst, peer):
        return pltpu.make_async_remote_copy(
            src_ref=src, dst_ref=dst, send_sem=ss.at[i], recv_sem=rs.at[i],
            device_id=peer, device_id_type=MESH,
        )

    x_p = remote(0, s_xp, r_xm, at(0, gxp))
    x_m = remote(1, s_xm, r_xp, at(0, gxm))
    t_p = [
        remote(2, s_pp, r_mm, at(1, gxp)),
        remote(3, s_pm, r_mp, at(1, gxm)),
        remote(4, px0.at[8:10], px0.at[0:2], at(1, c["gx"])),
        remote(5, eb.at[8:10, 0:64], eb.at[0:2, 0:64], at(1, c["gx"])),
        remote(6, mass.at[7], mm.at[0:64], at(1, c["gx"])),
        remote(7, pyo.at[0:64], pyl.at[0:64], at(1, c["gx"])),
    ]
    t_m = [
        remote(8, s_mp, r_pm, at(-1, gxp)),
        remote(9, s_mm, r_pp, at(-1, gxm)),
        remote(10, px0.at[2:5], px0.at[10:13], at(-1, c["gx"])),
        remote(11, eb.at[2:5, 0:64], eb.at[10:13, 0:64], at(-1, c["gx"])),
        remote(12, pyo.at[0:64], pyh.at[0:64], at(-1, c["gx"])),
    ]

    @pl.when(has_p)
    def _():
        for copy in t_p[:2]:
            copy.start()

    @pl.when(has_m)
    def _():
        for copy in t_m[:2]:
            copy.start()

    x_p.start()
    x_m.start()

    @pl.when(has_m)
    def _():
        for copy in t_m[2:]:
            copy.start()

    @pl.when(has_p)
    def _():
        for copy in t_p[2:]:
            copy.start()

    m0[0:64, :] = m7

    x_p.wait()
    x_m.wait()

    @pl.when(has_p)
    def _():
        for copy in t_p:
            copy.wait_send()

    @pl.when(has_m)
    def _():
        for copy in t_m:
            copy.wait_send()

    for t in range(8):
        eb[t + 2, 64:67, :] = r_xp[3 * t : 3 * t + 3, :]
        eb[t + 2, 70:72, :] = r_xm[2 * t : 2 * t + 2, :]
    pxm[2:10, :] = r_xm[16:24, :]
    m0[64:67, :] = r_xp[24:27, :]
    m0[70:72, :] = r_xm[24:26, :]
    pyo[64:67, :] = r_xp[27:30, :]
    pyo[70:72, :] = r_xm[26:28, :]

    @pl.when(has_m)
    def _():
        for copy in t_p:
            copy.wait_recv()
        for j in range(2):
            eb[j, 64:67, :] = r_mp[3 * j : 3 * j + 3, :]
            eb[j, 70:72, :] = r_mm[2 * j : 2 * j + 2, :]
        pxm[0:2, :] = r_mm[4:6, :]
        mm[64:67, :] = r_mp[6:9, :]
        mm[70:72, :] = r_mm[6:8, :]
        pyl[64:67, :] = r_mp[9:12, :]
        pyl[70:72, :] = r_mm[8:10, :]
        eb[2] = eb[2] - mm[...]

    @pl.when(has_p)
    def _():
        for copy in t_m:
            copy.wait_recv()
        for j in range(3):
            eb[10 + j, 64:67, :] = r_pp[3 * j : 3 * j + 3, :]
            eb[10 + j, 70:72, :] = r_pm[2 * j : 2 * j + 2, :]
        pxm[10:13, :] = r_pm[6:9, :]
        pyh[64:67, :] = r_pp[9:12, :]
        pyh[70:72, :] = r_pm[9:11, :]
        eb[10] = eb[10] - m0[...]

    for p in range(TP):
        eb[p, 0:1, :] = eb[p, 0:1, :] - pxm[p : p + 1, :]
        eb[p, 64:65, :] = eb[p, 64:65, :] - px0[p : p + 1, :]

    own = pyo[...]
    low = jnp.where(lane72 < 8, roll(own, 104, 1), roll(own, 120, 1))
    high = jnp.where(lane72 < 96, -roll(own, 16, 1), -roll(own, 32, 1))
    high = jnp.where(lane72 < 88, 0.0, high)
    low = jnp.where(has_m, roll(pyl[...], 64, 1), low)
    high = jnp.where(has_p, roll(pyh[...], 64, 1), high)
    py0 = jnp.where(lane72 < 16, low, jnp.where(lane72 < 80, own, high))

    @pl.when(jnp.logical_not(has_m))
    def _():
        eb[1] = eb[2]
        eb[0] = eb[3]

    @pl.when(jnp.logical_not(has_p))
    def _():
        eb[10] = jnp.zeros((XR, 128), F32)
        eb[11] = -eb[9]
        eb[12] = -eb[8]

    def pack(p, strips):
        v = eb[p]
        here = lane72 // 8 == p
        shifted = (roll(v, 8 * p + 2, 1), roll(v, 8 * p + 5, 1))
        return tuple(jnp.where(here, r, strip) for r, strip in zip(shifted, strips))

    zero8, zero72 = jnp.zeros((8, 128), F32), jnp.zeros((XR, 128), F32)
    left, right = zero72, zero72
    for p in range(TP):
        left, right = pack(p, (left, right))
    s_yp[...] = jnp.where(slot72 == 5, py0, right)
    s_ym[...] = left
    y_p = remote(13, s_yp, r_ym, (ta, c["gx"], gyp))
    y_m = remote(14, s_ym, r_yp, (ta, c["gx"], gym))
    y_p.start()
    y_m.start()

    def spread(src, dst):
        def step(p, _):
            v = src[p]
            ends = roll(v, 1, 1) + roll(v, 127, 1)
            dst[p] = (src[p - 1] + src[p + 1]) + (roll(v, 1, 0) + roll(v, XR - 1, 0)) + ends
            return 0

        return step

    def fold(v):
        return jnp.sum(v.reshape(8, 8, 128), axis=0)

    def moments(p, acc):
        b, u, full = eb[p, 0:64, :], e1[p, 0:64, :], e2[p]
        w = full[0:64]
        later = e2[p + 1, 0:64, :] + roll(full, XR - 1, 0)[0:64]
        terms = (b * b, b * u, u * u, u * w, w * w, w * later, w * roll(w, 127, 1))
        return tuple(a + fold(v) for a, v in zip(acc, terms))

    lax.fori_loop(1, 12, spread(eb, e1), 0)
    lax.fori_loop(2, 11, spread(e1, e2), 0)
    acc = lax.fori_loop(2, 10, moments, (zero8,) * 7)
    w0 = e2[2, 0:64, :]
    first = fold(w0 * w0)

    y_p.wait()
    y_m.wait()
    near = roll(r_ym[...], 125, 1)
    left = jnp.where(slot72 < 2, near, left) - jnp.where(slot72 == 2, near, 0.0)
    near = roll(r_yp[...], 3, 1)
    right = jnp.where(slot72 >= 5, near, right) - jnp.where(slot72 == 5, py0, 0.0)

    def around(v):
        return (
            (roll(v, 8, 1) + roll(v, 120, 1))
            + (roll(v, 1, 0) + roll(v, XR - 1, 0))
            + (roll(v, 1, 1) + roll(v, 127, 1))
        )

    strips = []
    inner = jnp.logical_and(lane8 >= 3, lane8 < 126)
    acc = [jnp.where(inner, v, 0.0) for v in acc[:6]] + [jnp.where(lane8 == 125, 0.0, jnp.where(inner, acc[6], 0.0))]
    first = jnp.where(inner, first, 0.0)
    block = jnp.logical_and(plane8 >= 2, plane8 < 10)
    for v, lo, hi in ((left, 2, 5), (right, 3, 5)):
        u = around(v)
        w = around(u)
        strips.append((v, u, w))
        later = (roll(w, 120, 1) + roll(w, XR - 1, 0))[0:64]
        v, u, w = v[0:64], u[0:64], w[0:64]
        cells = jnp.logical_and(block, jnp.logical_and(slot8 >= lo, slot8 < hi))
        pairs = jnp.logical_and(block, jnp.logical_and(slot8 >= 2, slot8 < 5))
        ww = fold(w * w)
        terms = [fold(e) for e in (v * v, v * u, u * u, u * w)] + [ww, fold(w * later)]
        acc = [a + jnp.where(cells, e, 0.0) for a, e in zip(acc, terms)] + [
            acc[6] + jnp.where(pairs, fold(w * roll(w, 127, 1)), 0.0)
        ]
        first = first + jnp.where(jnp.logical_and(cells, plane8 == 2), ww, 0.0)
    first = jnp.where(ta == 0, first, 0.0)
    acc = acc[:5] + [2.0 * (acc[5] + acc[6]) + first]
    lane1 = lax.broadcasted_iota(jnp.int32, (1, 128), 1)
    row = jnp.zeros((1, 128), F32)
    for i, v in enumerate(acc):
        row = jnp.where(lane1 == i, jnp.sum(v, keepdims=True), row)

    def send_all(buf, row, peers, send, recv):
        n = len(peers)
        buf[0] = row
        for i, peer in enumerate(peers):
            pltpu.make_async_remote_copy(
                src_ref=buf.at[0], dst_ref=buf.at[i + 1], send_sem=send, recv_sem=recv,
                device_id=peer, device_id_type=MESH,
            ).start()
        return pltpu.make_async_remote_copy(
            src_ref=buf.at[1 : n + 1], dst_ref=buf.at[1 : n + 1], send_sem=send, recv_sem=recv,
            device_id=peers[0], device_id_type=MESH,
        )

    def sum_all(buf, n):
        total = buf[0]
        for i in range(n):
            total = total + buf[i + 1]
        return total

    sent_a = send_all(buf_a, row, peers_a, ra_send, ra_recv)

    def differences(i, e):
        sl, sr = strips[0][i], strips[1][i]

        def whole(p):
            v = jnp.where(lane72 < 3, roll(sl, 126 - 8 * p, 1), e[p])
            return jnp.where(lane72 >= 126, roll(sr, 123 - 8 * p, 1), v)

        def step(t, v):
            p = t + 2
            nxt = whole(p + 1)
            v64 = v[0:64]
            hi = roll(jnp.where(lane64 == 0, roll(sr[0:64], 123 - 8 * p, 1), v64), 127, 1)
            diffs[i, 0, t] = v64 - nxt[0:64]
            diffs[i, 1, t] = v64 - roll(v, XR - 1, 0)[0:64]
            diffs[i, 2, t] = v64 - hi
            return nxt

        lax.fori_loop(0, 8, step, whole(2))

    for i, e in enumerate((eb, e1, e2)):
        differences(i, e)

    sent_a.wait_recv()
    row = sum_all(buf_a, len(peers_a))
    sent_b = send_all(buf_b, row, peers_b, rb_send, rb_recv)
    sent_b.wait_recv()
    row = sum_all(buf_b, len(peers_b))
    n = [jnp.sum(jnp.where(lane1 == i, row, 0.0), axis=1, keepdims=True) for i in range(6)]

    g0, g1, g2, g3, g4 = (6.0 * n[i] - n[i + 1] for i in range(5))
    l1, l2 = g1 / g0, g2 / g0
    d1 = g2 - l1 * g1
    f1 = g3 - l2 * g1
    l3 = f1 / d1
    d2 = g4 - l2 * g2 - l3 * f1
    y1 = n[1] - l1 * n[0]
    y2 = n[2] - l2 * n[0] - l3 * y1
    c2 = y2 / d2
    c1 = y1 / d1 - l3 * c2
    c0 = n[0] / g0 - l1 * c1 - l2 * c2
    c0, c1, c2 = (jnp.broadcast_to(v, (64, 128)) for v in (c0, c1, c2))

    def finish(t, _):
        for k, (old, out) in enumerate(((mass, mo_ref), (px, xo_ref), (py, yo_ref))):
            step = c0 * diffs[0, k, t] + c1 * diffs[1, k, t] + c2 * diffs[2, k, t]
            out[t] = old[t] - step
        return 0

    lax.fori_loop(0, 8, finish, 0)
    sent_a.wait_send()
    sent_b.wait_send()


def store(a_ref, b_ref, c_ref, a_out, b_out, c_out, sem):
    pairs = ((a_ref, a_out), (b_ref, b_out), (c_ref, c_out))
    copies = [pltpu.make_async_copy(src, dst, sem.at[i]) for i, (src, dst) in enumerate(pairs)]
    for copy in copies:
        copy.start()
    for copy in copies:
        copy.wait()


def body(density, flux_x, flux_y, congestion, initial_density):
    block = jax.ShapeDtypeStruct((8, 64, 128), F32)
    vm = lambda *s: pltpu.VMEM(s, F32)
    dma = pltpu.SemaphoreType.DMA
    arrays = (density, flux_x, flux_y, congestion, initial_density)
    arrays = [pltpu.with_memory_space_constraint(a, pltpu.HBM) for a in arrays]
    outs = pl.pallas_call(
        kernel,
        out_shape=(block,) * 3,
        in_specs=[pl.BlockSpec(memory_space=pltpu.HBM)] * 5,
        out_specs=[pl.BlockSpec(memory_space=pltpu.VMEM)] * 3,
        scratch_shapes=[vm(8, 64, 128)] * 4
        + [vm(64, 128)]
        + [vm(8, 64, 128)] * 3
        + [vm(TP, XR, 128)] * 3
        + [vm(16, 128)] * 2
        + [vm(XR, 128)] * 5
        + [vm(3, 3, 8, 64, 128)]
        + [vm(32, 128)] * 2
        + [vm(16, 128)] * 4
        + [vm(32, 128)] * 2
        + [vm(16, 128)] * 4
        + [vm(XR, 128)] * 4
        + [vm(16, 1, 128), vm(32, 1, 128)]
        + [dma((5,)), dma((15,)), dma((15,))]
        + [dma] * 4,
        compiler_params=pltpu.CompilerParams(
            collective_id=0, has_side_effects=True, vmem_limit_bytes=VMEM_MAIN
        ),
        name="prox_project",
    )(*arrays)
    return pl.pallas_call(
        store,
        out_shape=(block,) * 3,
        in_specs=[pl.BlockSpec(memory_space=pltpu.VMEM)] * 3,
        out_specs=[pl.BlockSpec(memory_space=pltpu.HBM)] * 3,
        scratch_shapes=[dma((3,))],
        compiler_params=pltpu.CompilerParams(vmem_limit_bytes=VMEM_STORE),
        name="store",
    )(*outs)


def solution(mesh):
    spec = P("ta", "gx", "gy")
    return jax.shard_map(
        body,
        mesh=mesh,
        in_specs=(spec,) * 4 + (P("gx", "gy"),),
        out_specs=(spec,) * 3,
        check_vma=False,
    )
```

```python
import functools
import itertools

import jax
import jax.numpy as jnp
from jax import lax
from jax.experimental import pallas as pl
from jax.experimental.pallas import tpu as pltpu
from jax.sharding import PartitionSpec as P

MESH = pl.DeviceIdType.MESH
NEWTON = 6
F32 = jnp.float32
TP, XR = 13, 72
VMEM_MAIN, VMEM_STORE = 16 * 2**20, 2**20


def roll(v, shift, axis):
    return pltpu.roll(v, shift, axis)


def group_a(c):
    peers = []
    for dz, dc in itertools.product(range(8), range(2)):
        if dz or dc:
            ta = c["ta"] + dc * (1 - 2 * lax.rem(c["ta"], 2))
            peers.append((min(dz, 8 - dz), (ta, c["gx"], lax.rem(c["gy"] + dz, 8))))
    return [p for _, p in sorted(peers, key=lambda e: -e[0])]


def group_b(c):
    y, x = (c["gx"] // 4) * 4 + c["ta"] // 2, lax.rem(c["gx"], 4)
    peers = []
    for dy, dx in itertools.product(range(8), range(4)):
        if dy or dx:
            yy, xx = lax.rem(y + dy, 8), lax.rem(x + dx, 4)
            at = (lax.rem(yy, 4) * 2 + lax.rem(c["ta"], 2), (yy // 4) * 4 + xx, c["gy"])
            peers.append((min(dy, 8 - dy) + min(dx, 4 - dx), at))
    return [p for _, p in sorted(peers, key=lambda e: -e[0])]


def kernel(
    d_hbm, fx_hbm, fy_hbm, c_hbm, i_hbm,
    mo_ref, xo_ref, yo_ref,
    d_ref, fx_ref, fy_ref, c_ref, i_ref, mass, px, py,
    eb, e1, e2, px0, pxm, m0, mm, pyo, pyl, pyh, diffs,
    s_xp, s_xm, s_pp, s_pm, s_mp, s_mm,
    r_xm, r_xp, r_mm, r_mp, r_pm, r_pp,
    s_yp, s_ym, r_ym, r_yp, buf_a, buf_b,
    in_sem, ss, rs, ra_send, ra_recv, rb_send, rb_recv, met,
):
    c = {a: lax.axis_index(a) for a in ("ta", "gx", "gy")}
    ta = c["ta"]
    has_m, has_p = ta > 0, ta < 7
    gxp, gxm = lax.rem(c["gx"] + 1, 8), lax.rem(c["gx"] + 7, 8)
    gyp, gym = lax.rem(c["gy"] + 1, 8), lax.rem(c["gy"] + 7, 8)
    peers_a, peers_b = group_a(c), group_b(c)

    def at(dt, gx):
        return (ta + dt, gx, c["gy"])

    loads = [
        pltpu.make_async_copy(a, b, in_sem.at[i])
        for i, (a, b) in enumerate(
            ((d_hbm, d_ref), (fx_hbm, fx_ref), (fy_hbm, fy_ref), (c_hbm, c_ref), (i_hbm, i_ref))
        )
    ]
    for copy in loads:
        copy.start()

    bar = pltpu.get_barrier_semaphore()

    def greet(peer):
        pl.semaphore_signal(bar, inc=1, device_id=peer, device_id_type=MESH)

    core, x, y = lax.rem(ta, 2), lax.rem(c["gx"], 4), (c["gx"] // 4) * 4 + ta // 2
    odd = core == 1
    away_p = jnp.logical_and(has_p, odd)
    away_m = jnp.logical_and(has_m, jnp.logical_not(odd))
    mate = at(1 - 2 * core, c["gx"])
    ring_x = [at(0, (c["gx"] // 4) * 4 + lax.rem(x + d, 4)) for d in (2, 1, 3)]
    ring_z = [(ta, c["gx"], lax.rem(c["gy"] + d, 8)) for d in (4, 3, 5, 2, 6, 1, 7)]
    ring_y = []
    for d in (4, 3, 5, 2, 6, 1, 7):
        yy = lax.rem(y + d, 8)
        ring_y.append((lax.rem(yy, 4) * 2 + core, (yy // 4) * 4 + x, c["gy"]))

    @pl.when(has_p)
    def _():
        greet(at(1, gxp))
        greet(at(1, gxm))

    @pl.when(has_m)
    def _():
        greet(at(-1, gxp))
        greet(at(-1, gxm))

    @pl.when(x == 3)
    def _():
        greet(at(0, gxp))

    @pl.when(x == 0)
    def _():
        greet(at(0, gxm))

    for peer in ring_y + ring_z + ring_x:
        greet(peer)

    @pl.when(away_p)
    def _():
        greet(at(1, c["gx"]))

    @pl.when(away_m)
    def _():
        greet(at(-1, c["gx"]))

    greet(mate)

    for copy in loads:
        copy.wait()

    lane64 = lax.broadcasted_iota(jnp.int32, (64, 128), 1)
    row64 = lax.broadcasted_iota(jnp.int32, (64, 128), 0)
    lane8 = lax.broadcasted_iota(jnp.int32, (8, 128), 1)
    lane72 = lax.broadcasted_iota(jnp.int32, (XR, 128), 1)
    slot8, plane8 = lax.rem(lane8, 8), lane8 // 8
    slot72 = lax.rem(lane72, 8)
    pyo[...] = jnp.zeros((XR, 128), F32)

    def newton(t, before):
        d, fx, fy = d_ref[t], fx_ref[t], fy_ref[t]
        q = fx * fx + fy * fy
        a = 1.0 + c_ref[t]
        m = (d + 0.5 * q) / (a + q)
        for _ in range(NEWTON - 1):
            s = m + 1.0
            s3 = s * s * s
            m = (d * s3 + q * (1.5 * s - 1.0)) / (a * s3 + q)
        shrink = m / (m + 1.0)
        vx, vy = fx * shrink, fy * shrink
        mass[t] = m
        px[t] = vx
        py[t] = vy
        b = m - before
        b = b + vx - jnp.where(row64 == 0, 0.0, roll(vx, 1, 0))
        b = b + vy - jnp.where(lane64 == 0, 0.0, roll(vy, 1, 1))
        eb[t + 2, 0:64, :] = b
        px0[pl.ds(t + 2, 1), :] = vx[63:64]
        pyo[0:64, :] = jnp.where(lane64 == 8 * t + 21, roll(vy, 8 * t + 22, 1), pyo[0:64, :])
        return m

    start = jnp.where(ta == 0, i_ref[...], 0.0)
    m7 = lax.fori_loop(0, 8, newton, start)

    for t in range(8):
        s_xp[2 * t : 2 * t + 2, :] = eb[t + 2, 62:64, :]
        s_xm[3 * t : 3 * t + 3, :] = eb[t + 2, 0:3, :]
    s_xp[16:24, :] = px0[2:10, :]
    s_xp[24:26, :] = m7[62:64]
    s_xp[26:28, :] = pyo[62:64, :]
    s_xm[24:27, :] = m7[0:3]
    s_xm[27:30, :] = pyo[0:3, :]
    s_pp[0:1, :] = eb[9, 63:64, :]
    s_pp[1:3, :] = px0[8:10, :]
    s_pp[3:5, :] = m7[62:64]
    s_pp[5:6, :] = pyo[63:64, :]
    s_pm[0:2, :] = eb[9, 0:2, :]
    s_pm[2:3, :] = eb[8, 0:1, :]
    s_pm[3:6, :] = m7[0:3]
    s_pm[6:8, :] = pyo[0:2, :]
    s_mp[0:2, :] = eb[2, 62:64, :]
    s_mp[2:3, :] = eb[3, 63:64, :]
    s_mp[3:6, :] = px0[2:5, :]
    s_mp[6:8, :] = pyo[62:64, :]
    s_mm[0:2, :] = eb[2, 0:2, :]
    s_mm[2:3, :] = eb[3, 0:1, :]
    s_mm[3:5, :] = pyo[0:2, :]

    def one(flag):
        return jnp.where(flag, 1, 0)

    greeted = len(ring_x + ring_y + ring_z) + 1 + 2 * one(has_p) + 2 * one(has_m)
    pl.semaphore_wait(bar, greeted + one(away_p) + one(away_m) + one(x == 3) + one(x == 0))

    def remote(i, src, dst, peer):
        return pltpu.make_async_remote_copy(
            src_ref=src, dst_ref=dst, send_sem=ss.at[i], recv_sem=rs.at[i],
            device_id=peer, device_id_type=MESH,
        )

    x_p = remote(0, s_xp, r_xm, at(0, gxp))
    x_m = remote(1, s_xm, r_xp, at(0, gxm))
    t_p = [
        remote(2, s_pp, r_mm, at(1, gxp)),
        remote(3, s_pm, r_mp, at(1, gxm)),
        remote(4, px0.at[8:10], px0.at[0:2], at(1, c["gx"])),
        remote(5, eb.at[8:10, 0:64], eb.at[0:2, 0:64], at(1, c["gx"])),
        remote(6, mass.at[7], mm.at[0:64], at(1, c["gx"])),
        remote(7, pyo.at[0:64], pyl.at[0:64], at(1, c["gx"])),
    ]
    t_m = [
        remote(8, s_mp, r_pm, at(-1, gxp)),
        remote(9, s_mm, r_pp, at(-1, gxm)),
        remote(10, px0.at[2:5], px0.at[10:13], at(-1, c["gx"])),
        remote(11, eb.at[2:5, 0:64], eb.at[10:13, 0:64], at(-1, c["gx"])),
        remote(12, pyo.at[0:64], pyh.at[0:64], at(-1, c["gx"])),
    ]

    @pl.when(has_p)
    def _():
        for copy in t_p[:2]:
            copy.start()

    @pl.when(has_m)
    def _():
        for copy in t_m[:2]:
            copy.start()

    x_p.start()
    x_m.start()

    @pl.when(has_m)
    def _():
        for copy in t_m[2:]:
            copy.start()

    @pl.when(has_p)
    def _():
        for copy in t_p[2:]:
            copy.start()

    for peer in ring_x + [mate]:
        pl.semaphore_signal(met, inc=1, device_id=peer, device_id_type=MESH)

    m0[0:64, :] = m7

    x_p.wait()
    x_m.wait()

    @pl.when(has_p)
    def _():
        for copy in t_p:
            copy.wait_send()

    @pl.when(has_m)
    def _():
        for copy in t_m:
            copy.wait_send()

    for t in range(8):
        eb[t + 2, 64:67, :] = r_xp[3 * t : 3 * t + 3, :]
        eb[t + 2, 70:72, :] = r_xm[2 * t : 2 * t + 2, :]
    pxm[2:10, :] = r_xm[16:24, :]
    m0[64:67, :] = r_xp[24:27, :]
    m0[70:72, :] = r_xm[24:26, :]
    pyo[64:67, :] = r_xp[27:30, :]
    pyo[70:72, :] = r_xm[26:28, :]

    @pl.when(has_m)
    def _():
        for copy in t_p:
            copy.wait_recv()
        eb[1, 71:72, :] = r_mm[0:1, :]
        pxm[0:2, :] = r_mm[1:3, :]
        mm[70:72, :] = r_mm[3:5, :]
        pyl[71:72, :] = r_mm[5:6, :]
        eb[1, 64:66, :] = r_mp[0:2, :]
        eb[0, 64:65, :] = r_mp[2:3, :]
        mm[64:67, :] = r_mp[3:6, :]
        pyl[64:66, :] = r_mp[6:8, :]
        eb[2] = eb[2] - mm[...]

    @pl.when(has_p)
    def _():
        for copy in t_m:
            copy.wait_recv()
        eb[10, 70:72, :] = r_pm[0:2, :]
        eb[11, 71:72, :] = r_pm[2:3, :]
        pxm[10:13, :] = r_pm[3:6, :]
        pyh[70:72, :] = r_pm[6:8, :]
        eb[10, 64:66, :] = r_pp[0:2, :]
        eb[11, 64:65, :] = r_pp[2:3, :]
        pyh[64:66, :] = r_pp[3:5, :]
        eb[10] = eb[10] - m0[...]

    for p in range(TP):
        eb[p, 0:1, :] = eb[p, 0:1, :] - pxm[p : p + 1, :]
        eb[p, 64:65, :] = eb[p, 64:65, :] - px0[p : p + 1, :]

    own = pyo[...]
    low = jnp.where(lane72 < 8, roll(own, 104, 1), roll(own, 120, 1))
    high = jnp.where(lane72 < 96, -roll(own, 16, 1), -roll(own, 32, 1))
    high = jnp.where(lane72 < 88, 0.0, high)
    low = jnp.where(has_m, roll(pyl[...], 64, 1), low)
    high = jnp.where(has_p, roll(pyh[...], 64, 1), high)
    py0 = jnp.where(lane72 < 16, low, jnp.where(lane72 < 80, own, high))

    @pl.when(jnp.logical_not(has_m))
    def _():
        eb[1] = eb[2]
        eb[0] = eb[3]

    @pl.when(jnp.logical_not(has_p))
    def _():
        eb[10] = jnp.zeros((XR, 128), F32)
        eb[11] = -eb[9]
        eb[12] = -eb[8]

    def pack(p, strips):
        v = eb[p]
        here = lane72 // 8 == p
        shifted = (roll(v, 8 * p + 2, 1), roll(v, 8 * p + 5, 1))
        return tuple(jnp.where(here, r, strip) for r, strip in zip(shifted, strips))

    zero8, zero72 = jnp.zeros((8, 128), F32), jnp.zeros((XR, 128), F32)
    left, right = zero72, zero72
    for p in range(TP):
        left, right = pack(p, (left, right))
    s_yp[...] = jnp.where(slot72 == 5, py0, right)
    s_ym[...] = left
    y_p = remote(13, s_yp, r_ym, (ta, c["gx"], gyp))
    y_m = remote(14, s_ym, r_yp, (ta, c["gx"], gym))
    y_p.start()
    y_m.start()

    def spread(src, dst):
        def step(p, _):
            v = src[p]
            ends = roll(v, 1, 1) + roll(v, 127, 1)
            dst[p] = (src[p - 1] + src[p + 1]) + (roll(v, 1, 0) + roll(v, XR - 1, 0)) + ends
            return 0

        return step

    def fold(v):
        return jnp.sum(v.reshape(8, 8, 128), axis=0)

    def moments(p, acc):
        b, u, full = eb[p, 0:64, :], e1[p, 0:64, :], e2[p]
        w = full[0:64]
        later = e2[p + 1, 0:64, :] + roll(full, XR - 1, 0)[0:64]
        terms = (b * b, b * u, u * u, u * w, w * w, w * later, w * roll(w, 127, 1))
        return tuple(a + fold(v) for a, v in zip(acc, terms))

    lax.fori_loop(1, 12, spread(eb, e1), 0)
    lax.fori_loop(2, 11, spread(e1, e2), 0)
    acc = lax.fori_loop(2, 10, moments, (zero8,) * 7)
    w0 = e2[2, 0:64, :]
    first = fold(w0 * w0)

    y_p.wait()
    y_m.wait()
    near = roll(r_ym[...], 125, 1)
    left = jnp.where(slot72 < 2, near, left) - jnp.where(slot72 == 2, near, 0.0)
    near = roll(r_yp[...], 3, 1)
    right = jnp.where(slot72 >= 5, near, right) - jnp.where(slot72 == 5, py0, 0.0)

    def around(v):
        return (
            (roll(v, 8, 1) + roll(v, 120, 1))
            + (roll(v, 1, 0) + roll(v, XR - 1, 0))
            + (roll(v, 1, 1) + roll(v, 127, 1))
        )

    strips = []
    inner = jnp.logical_and(lane8 >= 3, lane8 < 126)
    acc = [jnp.where(inner, v, 0.0) for v in acc[:6]] + [jnp.where(lane8 == 125, 0.0, jnp.where(inner, acc[6], 0.0))]
    first = jnp.where(inner, first, 0.0)
    block = jnp.logical_and(plane8 >= 2, plane8 < 10)
    for v, lo, hi in ((left, 2, 5), (right, 3, 5)):
        u = around(v)
        w = around(u)
        strips.append((v, u, w))
        later = (roll(w, 120, 1) + roll(w, XR - 1, 0))[0:64]
        v, u, w = v[0:64], u[0:64], w[0:64]
        cells = jnp.logical_and(block, jnp.logical_and(slot8 >= lo, slot8 < hi))
        pairs = jnp.logical_and(block, jnp.logical_and(slot8 >= 2, slot8 < 5))
        ww = fold(w * w)
        terms = [fold(e) for e in (v * v, v * u, u * u, u * w)] + [ww, fold(w * later)]
        acc = [a + jnp.where(cells, e, 0.0) for a, e in zip(acc, terms)] + [
            acc[6] + jnp.where(pairs, fold(w * roll(w, 127, 1)), 0.0)
        ]
        first = first + jnp.where(jnp.logical_and(cells, plane8 == 2), ww, 0.0)
    first = jnp.where(ta == 0, first, 0.0)
    acc = acc[:5] + [2.0 * (acc[5] + acc[6]) + first]
    lane1 = lax.broadcasted_iota(jnp.int32, (1, 128), 1)
    row = jnp.zeros((1, 128), F32)
    for i, v in enumerate(acc):
        row = jnp.where(lane1 == i, jnp.sum(v, keepdims=True), row)

    def send_all(buf, row, peers, send, recv):
        n = len(peers)
        buf[0] = row
        for i, peer in enumerate(peers):
            pltpu.make_async_remote_copy(
                src_ref=buf.at[0], dst_ref=buf.at[i + 1], send_sem=send, recv_sem=recv,
                device_id=peer, device_id_type=MESH,
            ).start()
        return pltpu.make_async_remote_copy(
            src_ref=buf.at[1 : n + 1], dst_ref=buf.at[1 : n + 1], send_sem=send, recv_sem=recv,
            device_id=peers[0], device_id_type=MESH,
        )

    def sum_all(buf, n):
        total = buf[0]
        for i in range(n):
            total = total + buf[i + 1]
        return total

    pl.semaphore_wait(met, len(ring_x) + 1)
    sent_a = send_all(buf_a, row, peers_a, ra_send, ra_recv)

    def differences(i, e):
        sl, sr = strips[0][i], strips[1][i]

        def whole(p):
            v = jnp.where(lane72 < 3, roll(sl, 126 - 8 * p, 1), e[p])
            return jnp.where(lane72 >= 126, roll(sr, 123 - 8 * p, 1), v)

        def step(t, v):
            p = t + 2
            nxt = whole(p + 1)
            v64 = v[0:64]
            hi = roll(jnp.where(lane64 == 0, roll(sr[0:64], 123 - 8 * p, 1), v64), 127, 1)
            diffs[i, 0, t] = v64 - nxt[0:64]
            diffs[i, 1, t] = v64 - roll(v, XR - 1, 0)[0:64]
            diffs[i, 2, t] = v64 - hi
            return nxt

        lax.fori_loop(0, 8, step, whole(2))

    for i, e in enumerate((eb, e1, e2)):
        differences(i, e)

    sent_a.wait_recv()
    row = sum_all(buf_a, len(peers_a))
    sent_b = send_all(buf_b, row, peers_b, rb_send, rb_recv)
    sent_b.wait_recv()
    row = sum_all(buf_b, len(peers_b))
    n = [jnp.sum(jnp.where(lane1 == i, row, 0.0), axis=1, keepdims=True) for i in range(6)]

    g0, g1, g2, g3, g4 = (6.0 * n[i] - n[i + 1] for i in range(5))
    l1, l2 = g1 / g0, g2 / g0
    d1 = g2 - l1 * g1
    f1 = g3 - l2 * g1
    l3 = f1 / d1
    d2 = g4 - l2 * g2 - l3 * f1
    y1 = n[1] - l1 * n[0]
    y2 = n[2] - l2 * n[0] - l3 * y1
    c2 = y2 / d2
    c1 = y1 / d1 - l3 * c2
    c0 = n[0] / g0 - l1 * c1 - l2 * c2
    c0, c1, c2 = (jnp.broadcast_to(v, (64, 128)) for v in (c0, c1, c2))

    def finish(t, _):
        for k, (old, out) in enumerate(((mass, mo_ref), (px, xo_ref), (py, yo_ref))):
            step = c0 * diffs[0, k, t] + c1 * diffs[1, k, t] + c2 * diffs[2, k, t]
            out[t] = old[t] - step
        return 0

    lax.fori_loop(0, 8, finish, 0)
    sent_a.wait_send()
    sent_b.wait_send()


def store(a_ref, b_ref, c_ref, a_out, b_out, c_out, sem):
    pairs = ((a_ref, a_out), (b_ref, b_out), (c_ref, c_out))
    copies = [pltpu.make_async_copy(src, dst, sem.at[i]) for i, (src, dst) in enumerate(pairs)]
    for copy in copies:
        copy.start()
    for copy in copies:
        copy.wait()


def body(density, flux_x, flux_y, congestion, initial_density):
    block = jax.ShapeDtypeStruct((8, 64, 128), F32)
    vm = lambda *s: pltpu.VMEM(s, F32)
    dma = pltpu.SemaphoreType.DMA
    arrays = (density, flux_x, flux_y, congestion, initial_density)
    arrays = [pltpu.with_memory_space_constraint(a, pltpu.HBM) for a in arrays]
    outs = pl.pallas_call(
        kernel,
        out_shape=(block,) * 3,
        in_specs=[pl.BlockSpec(memory_space=pltpu.HBM)] * 5,
        out_specs=[pl.BlockSpec(memory_space=pltpu.VMEM)] * 3,
        scratch_shapes=[vm(8, 64, 128)] * 4
        + [vm(64, 128)]
        + [vm(8, 64, 128)] * 3
        + [vm(TP, XR, 128)] * 3
        + [vm(16, 128)] * 2
        + [vm(XR, 128)] * 5
        + [vm(3, 3, 8, 64, 128)]
        + [vm(32, 128)] * 2
        + [vm(8, 128)] * 4
        + [vm(32, 128)] * 2
        + [vm(8, 128)] * 4
        + [vm(XR, 128)] * 4
        + [vm(16, 1, 128), vm(32, 1, 128)]
        + [dma((5,)), dma((15,)), dma((15,))]
        + [dma] * 4
        + [pltpu.SemaphoreType.REGULAR],
        compiler_params=pltpu.CompilerParams(
            collective_id=0, has_side_effects=True, vmem_limit_bytes=VMEM_MAIN
        ),
        name="prox_project",
    )(*arrays)
    return pl.pallas_call(
        store,
        out_shape=(block,) * 3,
        in_specs=[pl.BlockSpec(memory_space=pltpu.VMEM)] * 3,
        out_specs=[pl.BlockSpec(memory_space=pltpu.HBM)] * 3,
        scratch_shapes=[dma((3,))],
        compiler_params=pltpu.CompilerParams(vmem_limit_bytes=VMEM_STORE),
        name="store",
    )(*outs)


def solution(mesh):
    spec = P("ta", "gx", "gy")
    return jax.shard_map(
        body,
        mesh=mesh,
        in_specs=(spec,) * 4 + (P("gx", "gy"),),
        out_specs=(spec,) * 3,
        check_vma=False,
    )
```

```python
import functools
import itertools

import jax
import jax.numpy as jnp
from jax import lax
from jax.experimental import pallas as pl
from jax.experimental.pallas import tpu as pltpu
from jax.sharding import PartitionSpec as P

MESH = pl.DeviceIdType.MESH
NEWTON = 6
F32 = jnp.float32
TP, XR = 13, 72
SHIFT, SHIFTS = 4.0, 4
VMEM_MAIN, VMEM_STORE = 16 * 2**20, 2**20


def roll(v, shift, axis):
    return pltpu.roll(v, shift, axis)


def group_a(c):
    peers = []
    for dz, dc in itertools.product(range(8), range(2)):
        if dz or dc:
            ta = c["ta"] + dc * (1 - 2 * lax.rem(c["ta"], 2))
            peers.append((min(dz, 8 - dz), (ta, c["gx"], lax.rem(c["gy"] + dz, 8))))
    return [p for _, p in sorted(peers, key=lambda e: -e[0])]


def group_b(c):
    y, x = (c["gx"] // 4) * 4 + c["ta"] // 2, lax.rem(c["gx"], 4)
    peers = []
    for dy, dx in itertools.product(range(8), range(4)):
        if dy or dx:
            yy, xx = lax.rem(y + dy, 8), lax.rem(x + dx, 4)
            at = (lax.rem(yy, 4) * 2 + lax.rem(c["ta"], 2), (yy // 4) * 4 + xx, c["gy"])
            peers.append((min(dy, 8 - dy) + min(dx, 4 - dx), at))
    return [p for _, p in sorted(peers, key=lambda e: -e[0])]


def kernel(
    d_hbm, fx_hbm, fy_hbm, c_hbm, i_hbm,
    mo_ref, xo_ref, yo_ref,
    d_ref, fx_ref, fy_ref, c_ref, i_ref, mass, px, py,
    eb, e1, e2, px0, pxm, m0, mm, pyo, pyl, pyh, diffs,
    s_xp, s_xm, s_pp, s_pm, s_mp, s_mm,
    r_xm, r_xp, r_mm, r_mp, r_pm, r_pp,
    s_yp, s_ym, r_ym, r_yp, buf_a, buf_b,
    in_sem, ss, rs, ra_send, ra_recv, rb_send, rb_recv, met,
):
    c = {a: lax.axis_index(a) for a in ("ta", "gx", "gy")}
    ta = c["ta"]
    has_m, has_p = ta > 0, ta < 7
    gxp, gxm = lax.rem(c["gx"] + 1, 8), lax.rem(c["gx"] + 7, 8)
    gyp, gym = lax.rem(c["gy"] + 1, 8), lax.rem(c["gy"] + 7, 8)
    peers_a, peers_b = group_a(c), group_b(c)

    def at(dt, gx):
        return (ta + dt, gx, c["gy"])

    bar = pltpu.get_barrier_semaphore()

    def greet(peer):
        pl.semaphore_signal(bar, inc=1, device_id=peer, device_id_type=MESH)

    core, x, y = lax.rem(ta, 2), lax.rem(c["gx"], 4), (c["gx"] // 4) * 4 + ta // 2
    odd = core == 1
    away_p = jnp.logical_and(has_p, odd)
    away_m = jnp.logical_and(has_m, jnp.logical_not(odd))
    mate = at(1 - 2 * core, c["gx"])
    ring_x = [at(0, (c["gx"] // 4) * 4 + lax.rem(x + d, 4)) for d in (2, 1, 3)]
    ring_z = [(ta, c["gx"], lax.rem(c["gy"] + d, 8)) for d in (4, 3, 5, 2, 6, 1, 7)]
    ring_y = []
    for d in (4, 3, 5, 2, 6, 1, 7):
        yy = lax.rem(y + d, 8)
        ring_y.append((lax.rem(yy, 4) * 2 + core, (yy // 4) * 4 + x, c["gy"]))

    @pl.when(has_p)
    def _():
        greet(at(1, gxp))
        greet(at(1, gxm))

    @pl.when(has_m)
    def _():
        greet(at(-1, gxp))
        greet(at(-1, gxm))

    @pl.when(x == 3)
    def _():
        greet(at(0, gxp))

    @pl.when(x == 0)
    def _():
        greet(at(0, gxm))

    loads = [
        pltpu.make_async_copy(a, b, in_sem.at[i])
        for i, (a, b) in enumerate(
            ((d_hbm, d_ref), (fx_hbm, fx_ref), (fy_hbm, fy_ref), (c_hbm, c_ref), (i_hbm, i_ref))
        )
    ]
    for copy in loads:
        copy.start()

    for peer in ring_y + ring_z + ring_x:
        greet(peer)

    @pl.when(away_p)
    def _():
        greet(at(1, c["gx"]))

    @pl.when(away_m)
    def _():
        greet(at(-1, c["gx"]))

    greet(mate)

    for copy in loads:
        copy.wait()

    lane64 = lax.broadcasted_iota(jnp.int32, (64, 128), 1)
    row64 = lax.broadcasted_iota(jnp.int32, (64, 128), 0)
    lane8 = lax.broadcasted_iota(jnp.int32, (8, 128), 1)
    lane72 = lax.broadcasted_iota(jnp.int32, (XR, 128), 1)
    slot8, plane8 = lax.rem(lane8, 8), lane8 // 8
    slot72 = lax.rem(lane72, 8)
    pyo[...] = jnp.zeros((XR, 128), F32)

    def newton(t, before):
        d, fx, fy = d_ref[t], fx_ref[t], fy_ref[t]
        q = fx * fx + fy * fy
        a = 1.0 + c_ref[t]
        m = (d + 0.5 * q) / (a + q)
        for _ in range(NEWTON - 1):
            s = m + 1.0
            s3 = s * s * s
            m = (d * s3 + q * (1.5 * s - 1.0)) / (a * s3 + q)
        shrink = m / (m + 1.0)
        vx, vy = fx * shrink, fy * shrink
        mass[t] = m
        px[t] = vx
        py[t] = vy
        b = m - before
        b = b + vx - jnp.where(row64 == 0, 0.0, roll(vx, 1, 0))
        b = b + vy - jnp.where(lane64 == 0, 0.0, roll(vy, 1, 1))
        eb[t + 2, 0:64, :] = b
        px0[pl.ds(t + 2, 1), :] = vx[63:64]
        pyo[0:64, :] = jnp.where(lane64 == 8 * t + 21, roll(vy, 8 * t + 22, 1), pyo[0:64, :])
        return m

    start = jnp.where(ta == 0, i_ref[...], 0.0)
    m7 = lax.fori_loop(0, 8, newton, start)

    for t in range(8):
        s_xp[2 * t : 2 * t + 2, :] = eb[t + 2, 62:64, :]
        s_xm[3 * t : 3 * t + 3, :] = eb[t + 2, 0:3, :]
    s_xp[16:24, :] = px0[2:10, :]
    s_xp[24:26, :] = m7[62:64]
    s_xp[26:28, :] = pyo[62:64, :]
    s_xm[24:27, :] = m7[0:3]
    s_xm[27:30, :] = pyo[0:3, :]
    s_pp[0:1, :] = eb[9, 63:64, :]
    s_pp[1:3, :] = px0[8:10, :]
    s_pp[3:5, :] = m7[62:64]
    s_pp[5:6, :] = pyo[63:64, :]
    s_pm[0:2, :] = eb[9, 0:2, :]
    s_pm[2:3, :] = eb[8, 0:1, :]
    s_pm[3:6, :] = m7[0:3]
    s_pm[6:8, :] = pyo[0:2, :]
    s_mp[0:2, :] = eb[2, 62:64, :]
    s_mp[2:3, :] = eb[3, 63:64, :]
    s_mp[3:6, :] = px0[2:5, :]
    s_mp[6:8, :] = pyo[62:64, :]
    s_mm[0:2, :] = eb[2, 0:2, :]
    s_mm[2:3, :] = eb[3, 0:1, :]
    s_mm[3:5, :] = pyo[0:2, :]

    def one(flag):
        return jnp.where(flag, 1, 0)

    greeted = len(ring_x + ring_y + ring_z) + 1 + 2 * one(has_p) + 2 * one(has_m)
    pl.semaphore_wait(bar, greeted + one(away_p) + one(away_m) + one(x == 3) + one(x == 0))

    def remote(i, src, dst, peer):
        return pltpu.make_async_remote_copy(
            src_ref=src, dst_ref=dst, send_sem=ss.at[i], recv_sem=rs.at[i],
            device_id=peer, device_id_type=MESH,
        )

    x_p = remote(0, s_xp, r_xm, at(0, gxp))
    x_m = remote(1, s_xm, r_xp, at(0, gxm))
    t_p = [
        remote(2, s_pp, r_mm, at(1, gxp)),
        remote(3, s_pm, r_mp, at(1, gxm)),
        remote(4, px0.at[8:10], px0.at[0:2], at(1, c["gx"])),
        remote(5, eb.at[8:10, 0:64], eb.at[0:2, 0:64], at(1, c["gx"])),
        remote(6, mass.at[7], mm.at[0:64], at(1, c["gx"])),
        remote(7, pyo.at[0:64], pyl.at[0:64], at(1, c["gx"])),
    ]
    t_m = [
        remote(8, s_mp, r_pm, at(-1, gxp)),
        remote(9, s_mm, r_pp, at(-1, gxm)),
        remote(10, px0.at[2:5], px0.at[10:13], at(-1, c["gx"])),
        remote(11, eb.at[2:5, 0:64], eb.at[10:13, 0:64], at(-1, c["gx"])),
        remote(12, pyo.at[0:64], pyh.at[0:64], at(-1, c["gx"])),
    ]

    @pl.when(has_p)
    def _():
        for copy in t_p[:2]:
            copy.start()

    @pl.when(has_m)
    def _():
        for copy in t_m[:2]:
            copy.start()

    x_p.start()
    x_m.start()

    @pl.when(has_m)
    def _():
        for copy in t_m[2:]:
            copy.start()

    @pl.when(has_p)
    def _():
        for copy in t_p[2:]:
            copy.start()

    for peer in ring_x + [mate]:
        pl.semaphore_signal(met, inc=1, device_id=peer, device_id_type=MESH)

    m0[0:64, :] = m7

    x_p.wait()
    x_m.wait()

    @pl.when(has_p)
    def _():
        for copy in t_p:
            copy.wait_send()

    @pl.when(has_m)
    def _():
        for copy in t_m:
            copy.wait_send()

    for t in range(8):
        eb[t + 2, 64:67, :] = r_xp[3 * t : 3 * t + 3, :]
        eb[t + 2, 70:72, :] = r_xm[2 * t : 2 * t + 2, :]
    pxm[2:10, :] = r_xm[16:24, :]
    m0[64:67, :] = r_xp[24:27, :]
    m0[70:72, :] = r_xm[24:26, :]
    pyo[64:67, :] = r_xp[27:30, :]
    pyo[70:72, :] = r_xm[26:28, :]

    @pl.when(has_m)
    def _():
        for copy in t_p:
            copy.wait_recv()
        eb[1, 71:72, :] = r_mm[0:1, :]
        pxm[0:2, :] = r_mm[1:3, :]
        mm[70:72, :] = r_mm[3:5, :]
        pyl[71:72, :] = r_mm[5:6, :]
        eb[1, 64:66, :] = r_mp[0:2, :]
        eb[0, 64:65, :] = r_mp[2:3, :]
        mm[64:67, :] = r_mp[3:6, :]
        pyl[64:66, :] = r_mp[6:8, :]
        eb[2] = eb[2] - mm[...]

    @pl.when(has_p)
    def _():
        for copy in t_m:
            copy.wait_recv()
        eb[10, 70:72, :] = r_pm[0:2, :]
        eb[11, 71:72, :] = r_pm[2:3, :]
        pxm[10:13, :] = r_pm[3:6, :]
        pyh[70:72, :] = r_pm[6:8, :]
        eb[10, 64:66, :] = r_pp[0:2, :]
        eb[11, 64:65, :] = r_pp[2:3, :]
        pyh[64:66, :] = r_pp[3:5, :]
        eb[10] = eb[10] - m0[...]

    for p in range(TP):
        eb[p, 0:1, :] = eb[p, 0:1, :] - pxm[p : p + 1, :]
        eb[p, 64:65, :] = eb[p, 64:65, :] - px0[p : p + 1, :]

    own = pyo[...]
    low = jnp.where(lane72 < 8, roll(own, 104, 1), roll(own, 120, 1))
    high = jnp.where(lane72 < 96, -roll(own, 16, 1), -roll(own, 32, 1))
    high = jnp.where(lane72 < 88, 0.0, high)
    low = jnp.where(has_m, roll(pyl[...], 64, 1), low)
    high = jnp.where(has_p, roll(pyh[...], 64, 1), high)
    py0 = jnp.where(lane72 < 16, low, jnp.where(lane72 < 80, own, high))

    @pl.when(jnp.logical_not(has_m))
    def _():
        eb[1] = eb[2]
        eb[0] = eb[3]

    @pl.when(jnp.logical_not(has_p))
    def _():
        eb[10] = jnp.zeros((XR, 128), F32)
        eb[11] = -eb[9]
        eb[12] = -eb[8]

    def pack(p, strips):
        v = eb[p]
        here = lane72 // 8 == p
        shifted = (roll(v, 8 * p + 2, 1), roll(v, 8 * p + 5, 1))
        return tuple(jnp.where(here, r, strip) for r, strip in zip(shifted, strips))

    zero8, zero72 = jnp.zeros((8, 128), F32), jnp.zeros((XR, 128), F32)
    left, right = zero72, zero72
    for p in range(TP):
        left, right = pack(p, (left, right))
    half = lax.rem(lax.broadcasted_iota(jnp.int32, (32, 128), 1), 8) < 4
    v = roll(jnp.where(slot72 == 5, py0, right), 125, 1)
    s_yp[0:32, :] = jnp.where(half, v[0:32], roll(v[40:72], 4, 1))
    s_yp[32:40, :] = v[32:40]
    v = roll(left, 3, 1)
    s_ym[0:32, :] = jnp.where(half, roll(v[40:72], 124, 1), v[0:32])
    s_ym[32:40, :] = v[32:40]
    y_p = remote(13, s_yp, r_ym, (ta, c["gx"], gyp))
    y_m = remote(14, s_ym, r_yp, (ta, c["gx"], gym))
    y_p.start()
    y_m.start()

    def spread(src, dst):
        def step(p, _):
            v = src[p]
            ends = roll(v, 1, 1) + roll(v, 127, 1)
            near = (src[p - 1] + src[p + 1]) + (roll(v, 1, 0) + roll(v, XR - 1, 0)) + ends
            dst[p] = 6.0 * v - near
            return 0

        return step

    def fold(v):
        return jnp.sum(v.reshape(8, 8, 128), axis=0)

    def shifted(b, u, w, k):
        v = u - k * SHIFT * b
        return v, (w - k * SHIFT * u) - k * SHIFT * v

    def edges(w, later):
        dx, dy = w - roll(w, XR - 1, 0), w - roll(w, 127, 1)
        dt, dx, dy = w[0:64] - later, dx[0:64], dy[0:64]
        return fold(dt * dt + dx * dx), fold(dy * dy)

    def moments(p, acc):
        here, nxt = (eb[p], e1[p], e2[p]), (eb[p + 1, 0:64, :], e1[p + 1, 0:64, :], e2[p + 1, 0:64, :])
        b = here[0][0:64]
        terms = [fold(b * b)]
        for k in range(SHIFTS):
            v, w = shifted(*here, k)
            e = edges(w, shifted(*nxt, k)[1])
            v, w = v[0:64], w[0:64]
            terms += [fold(b * v), fold(v * v), fold(v * w), fold(w * w), *e]
        return tuple(a + t for a, t in zip(acc, terms))

    for p in range(1, 12):
        spread(eb, e1)(p, 0)
    for p in range(2, 11):
        spread(e1, e2)(p, 0)
    acc = lax.fori_loop(2, 10, moments, (zero8,) * (1 + 6 * SHIFTS))

    y_p.wait()
    y_m.wait()
    v = r_ym[...]
    near = jnp.concatenate([v, roll(v[0:32], 124, 1)], 0)
    left = jnp.where(slot72 < 2, near, left) - jnp.where(slot72 == 2, near, 0.0)
    v = r_yp[...]
    near = jnp.concatenate([v, roll(v[0:32], 4, 1)], 0)
    right = jnp.where(slot72 >= 5, near, right) - jnp.where(slot72 == 5, py0, 0.0)

    def apply(v):
        return 6.0 * v - (
            (roll(v, 8, 1) + roll(v, 120, 1))
            + (roll(v, 1, 0) + roll(v, XR - 1, 0))
            + (roll(v, 1, 1) + roll(v, 127, 1))
        )

    inner = jnp.logical_and(lane8 >= 3, lane8 < 126)
    inner_y = jnp.logical_and(lane8 >= 3, lane8 < 125)
    masks = [inner] + ([inner] * 5 + [inner_y]) * SHIFTS
    acc = [jnp.where(mask, v, 0.0) for mask, v in zip(masks, acc)]
    block = jnp.logical_and(plane8 >= 2, plane8 < 10)
    pairs = jnp.logical_and(block, jnp.logical_and(slot8 >= 2, slot8 < 5))
    strips = []
    for b, lo in ((left, 2), (right, 3)):
        u = apply(b)
        strips.append((b, u, apply(u)))
        cells = jnp.logical_and(block, jnp.logical_and(slot8 >= lo, slot8 < 5))
        b64 = b[0:64]
        terms = [fold(b64 * b64)]
        for k in range(SHIFTS):
            v, w = shifted(*strips[-1], k)
            e = edges(w, roll(w, 120, 1)[0:64])
            v, w = v[0:64], w[0:64]
            terms += [fold(b64 * v), fold(v * v), fold(v * w), fold(w * w), *e]
        masks = [cells] + ([cells] * 5 + [pairs]) * SHIFTS
        acc = [a + jnp.where(mask, e, 0.0) for a, mask, e in zip(acc, masks, terms)]
    sub8 = lax.broadcasted_iota(jnp.int32, (8, 128), 0)
    spot = zero8
    for j in range(6):
        rows = zero8
        for k in range(SHIFTS):
            v = acc[0] if j == 0 else acc[6 * k + j]
            if j == 5:
                v = v + acc[6 * k + 6]
            rows = jnp.where(sub8 == k, jnp.sum(v, axis=0, keepdims=True), rows)
        spot = jnp.where(lane8 == 8 * j + sub8, jnp.sum(rows, axis=1, keepdims=True), spot)
    row = jnp.sum(spot, axis=0, keepdims=True)

    def send_all(buf, row, peers, send, recv):
        n = len(peers)
        buf[0] = row
        for i, peer in enumerate(peers):
            pltpu.make_async_remote_copy(
                src_ref=buf.at[0], dst_ref=buf.at[i + 1], send_sem=send, recv_sem=recv,
                device_id=peer, device_id_type=MESH,
            ).start()
        return pltpu.make_async_remote_copy(
            src_ref=buf.at[1 : n + 1], dst_ref=buf.at[1 : n + 1], send_sem=send, recv_sem=recv,
            device_id=peers[0], device_id_type=MESH,
        )

    def sum_all(buf, n):
        total = buf[0]
        for i in range(n):
            total = total + buf[i + 1]
        return total

    pl.semaphore_wait(met, len(ring_x) + 1)
    sent_a = send_all(buf_a, row, peers_a, ra_send, ra_recv)

    def differences(i, e):
        sl, sr = strips[0][i], strips[1][i]

        def whole(p):
            v = jnp.where(lane72 < 3, roll(sl, 126 - 8 * p, 1), e[p])
            return jnp.where(lane72 >= 126, roll(sr, 123 - 8 * p, 1), v)

        def step(t, v):
            p = t + 2
            nxt = whole(p + 1)
            v64 = v[0:64]
            hi = roll(jnp.where(lane64 == 0, roll(sr[0:64], 123 - 8 * p, 1), v64), 127, 1)
            diffs[i, 0, t] = v64 - nxt[0:64]
            diffs[i, 1, t] = v64 - roll(v, XR - 1, 0)[0:64]
            diffs[i, 2, t] = v64 - hi
            return nxt

        lax.fori_loop(0, 8, step, whole(2))

    for i, e in enumerate((eb, e1, e2)):
        differences(i, e)

    sent_a.wait_recv()
    row = sum_all(buf_a, len(peers_a))
    sent_b = send_all(buf_b, row, peers_b, rb_send, rb_recv)
    sent_b.wait_recv()
    row = sum_all(buf_b, len(peers_b))
    row = jnp.broadcast_to(row, (8, 128))
    m0, m1, m2, m3, m4, g4 = (row if j == 0 else roll(row, 128 - 8 * j, 1) for j in range(6))
    shift = SHIFT * lane8.astype(F32)
    g0, g1, g2, g3 = shift * m0 + m1, shift * m1 + m2, shift * m2 + m3, shift * m3 + m4
    l1, l2 = g1 / g0, g2 / g0
    d1 = g2 - l1 * g1
    f1 = g3 - l2 * g1
    i1 = jnp.where(d1 > 0.0, 1.0 / d1, 0.0)
    l3 = f1 * i1
    d2 = g4 - l2 * g2 - l3 * f1
    y1 = m1 - l1 * m0
    y2 = m2 - l2 * m0 - l3 * y1
    c2 = jnp.where(d2 > 0.0, y2 / d2, 0.0)
    c1 = y1 * i1 - l3 * c2
    c0 = m0 / g0 - l1 * c1 - l2 * c2
    c0, c1 = c0 - shift * (c1 - shift * c2), c1 - 2.0 * shift * c2
    far = jnp.where(lane8 < SHIFTS, jnp.abs(m1), jnp.inf)
    best = far == jnp.min(far, axis=1, keepdims=True)
    count = jnp.sum(jnp.where(best, 1.0, 0.0), axis=1, keepdims=True)
    c0, c1, c2 = (
        jnp.sum(jnp.where(best, v, 0.0), axis=1, keepdims=True) / count for v in (c0, c1, c2)
    )
    c0, c1, c2 = (jnp.broadcast_to(v[0:1], (64, 128)) for v in (c0, c1, c2))

    def finish(t, _):
        for k, (old, out) in enumerate(((mass, mo_ref), (px, xo_ref), (py, yo_ref))):
            step = c0 * diffs[0, k, t] + c1 * diffs[1, k, t] + c2 * diffs[2, k, t]
            out[t] = old[t] - step
        return 0

    lax.fori_loop(0, 8, finish, 0)
    sent_a.wait_send()
    sent_b.wait_send()


def store(a_ref, b_ref, c_ref, a_out, b_out, c_out, sem):
    pairs = ((a_ref, a_out), (b_ref, b_out), (c_ref, c_out))
    copies = [pltpu.make_async_copy(src, dst, sem.at[i]) for i, (src, dst) in enumerate(pairs)]
    for copy in copies:
        copy.start()
    for copy in copies:
        copy.wait()


def body(density, flux_x, flux_y, congestion, initial_density):
    block = jax.ShapeDtypeStruct((8, 64, 128), F32)
    vm = lambda *s: pltpu.VMEM(s, F32)
    dma = pltpu.SemaphoreType.DMA
    arrays = (density, flux_x, flux_y, congestion, initial_density)
    arrays = [pltpu.with_memory_space_constraint(a, pltpu.HBM) for a in arrays]
    outs = pl.pallas_call(
        kernel,
        out_shape=(block,) * 3,
        in_specs=[pl.BlockSpec(memory_space=pltpu.HBM)] * 5,
        out_specs=[pl.BlockSpec(memory_space=pltpu.VMEM)] * 3,
        scratch_shapes=[vm(8, 64, 128)] * 4
        + [vm(64, 128)]
        + [vm(8, 64, 128)] * 3
        + [vm(TP, XR, 128)] * 3
        + [vm(16, 128)] * 2
        + [vm(XR, 128)] * 5
        + [vm(3, 3, 8, 64, 128)]
        + [vm(32, 128)] * 2
        + [vm(8, 128)] * 4
        + [vm(32, 128)] * 2
        + [vm(8, 128)] * 4
        + [vm(40, 128)] * 4
        + [vm(16, 1, 128), vm(32, 1, 128)]
        + [dma((5,)), dma((15,)), dma((15,))]
        + [dma] * 4
        + [pltpu.SemaphoreType.REGULAR],
        compiler_params=pltpu.CompilerParams(
            collective_id=0, has_side_effects=True, vmem_limit_bytes=VMEM_MAIN
        ),
        name="prox_project",
    )(*arrays)
    return pl.pallas_call(
        store,
        out_shape=(block,) * 3,
        in_specs=[pl.BlockSpec(memory_space=pltpu.VMEM)] * 3,
        out_specs=[pl.BlockSpec(memory_space=pltpu.HBM)] * 3,
        scratch_shapes=[dma((3,))],
        compiler_params=pltpu.CompilerParams(vmem_limit_bytes=VMEM_STORE),
        name="store",
    )(*outs)


def solution(mesh):
    spec = P("ta", "gx", "gy")
    return jax.shard_map(
        body,
        mesh=mesh,
        in_specs=(spec,) * 4 + (P("gx", "gy"),),
        out_specs=(spec,) * 3,
        check_vma=False,
    )
```

```python
import functools
import itertools

import jax
import jax.numpy as jnp
from jax import lax
from jax.experimental import pallas as pl
from jax.experimental.pallas import tpu as pltpu
from jax.sharding import PartitionSpec as P

MESH = pl.DeviceIdType.MESH
NEWTON = 6
F32 = jnp.float32
TP, XR = 13, 72
SHIFT, SHIFTS = 4.0, 4
VMEM_MAIN, VMEM_STORE = 16 * 2**20, 4 * 2**20


def roll(v, shift, axis):
    return pltpu.roll(v, shift, axis)


def group_a(c):
    peers = []
    for dz, dc in itertools.product(range(8), range(2)):
        if dz or dc:
            ta = c["ta"] + dc * (1 - 2 * lax.rem(c["ta"], 2))
            peers.append((min(dz, 8 - dz), (ta, c["gx"], lax.rem(c["gy"] + dz, 8))))
    return [p for _, p in sorted(peers, key=lambda e: -e[0])]


def group_b(c):
    y, x = (c["gx"] // 4) * 4 + c["ta"] // 2, lax.rem(c["gx"], 4)
    peers = []
    for dy, dx in itertools.product(range(8), range(4)):
        if dy or dx:
            yy, xx = lax.rem(y + dy, 8), lax.rem(x + dx, 4)
            at = (lax.rem(yy, 4) * 2 + lax.rem(c["ta"], 2), (yy // 4) * 4 + xx, c["gy"])
            peers.append((min(dy, 8 - dy) + min(dx, 4 - dx), at))
    return [p for _, p in sorted(peers, key=lambda e: -e[0])]


def kernel(
    d_hbm, fx_hbm, fy_hbm, c_hbm, i_hbm,
    mass, px, py, diffs, coef,
    d_ref, fx_ref, fy_ref, c_ref, i_ref,
    eb, e1, e2, px0, pxm, m0, mm, pyo, pyl, pyh,
    s_xp, s_xm, s_pp, s_pm, s_mp, s_mm,
    r_xm, r_xp, r_mm, r_mp, r_pm, r_pp,
    s_yp, s_ym, r_ym, r_yp, buf_a, buf_b,
    in_sem, ss, rs, ra_send, ra_recv, rb_send, rb_recv, met,
):
    c = {a: lax.axis_index(a) for a in ("ta", "gx", "gy")}
    ta = c["ta"]
    has_m, has_p = ta > 0, ta < 7
    gxp, gxm = lax.rem(c["gx"] + 1, 8), lax.rem(c["gx"] + 7, 8)
    gyp, gym = lax.rem(c["gy"] + 1, 8), lax.rem(c["gy"] + 7, 8)
    peers_a, peers_b = group_a(c), group_b(c)

    def at(dt, gx):
        return (ta + dt, gx, c["gy"])

    bar = pltpu.get_barrier_semaphore()

    def greet(peer):
        pl.semaphore_signal(bar, inc=1, device_id=peer, device_id_type=MESH)

    core, x, y = lax.rem(ta, 2), lax.rem(c["gx"], 4), (c["gx"] // 4) * 4 + ta // 2
    odd = core == 1
    away_p = jnp.logical_and(has_p, odd)
    away_m = jnp.logical_and(has_m, jnp.logical_not(odd))
    mate = at(1 - 2 * core, c["gx"])
    ring_x = [at(0, (c["gx"] // 4) * 4 + lax.rem(x + d, 4)) for d in (2, 1, 3)]
    ring_z = [(ta, c["gx"], lax.rem(c["gy"] + d, 8)) for d in (4, 3, 5, 2, 6, 1, 7)]
    ring_y = []
    for d in (4, 3, 5, 2, 6, 1, 7):
        yy = lax.rem(y + d, 8)
        ring_y.append((lax.rem(yy, 4) * 2 + core, (yy // 4) * 4 + x, c["gy"]))

    @pl.when(has_p)
    def _():
        greet(at(1, gxp))
        greet(at(1, gxm))

    @pl.when(has_m)
    def _():
        greet(at(-1, gxp))
        greet(at(-1, gxm))

    @pl.when(x == 3)
    def _():
        greet(at(0, gxp))

    @pl.when(x == 0)
    def _():
        greet(at(0, gxm))

    loads = [
        pltpu.make_async_copy(a, b, in_sem.at[i])
        for i, (a, b) in enumerate(
            ((d_hbm, d_ref), (fx_hbm, fx_ref), (fy_hbm, fy_ref), (c_hbm, c_ref), (i_hbm, i_ref))
        )
    ]
    for copy in loads:
        copy.start()

    for peer in ring_y + ring_z + ring_x:
        greet(peer)

    @pl.when(away_p)
    def _():
        greet(at(1, c["gx"]))

    @pl.when(away_m)
    def _():
        greet(at(-1, c["gx"]))

    greet(mate)

    for copy in loads:
        copy.wait()

    lane64 = lax.broadcasted_iota(jnp.int32, (64, 128), 1)
    row64 = lax.broadcasted_iota(jnp.int32, (64, 128), 0)
    lane8 = lax.broadcasted_iota(jnp.int32, (8, 128), 1)
    lane72 = lax.broadcasted_iota(jnp.int32, (XR, 128), 1)
    slot8, plane8 = lax.rem(lane8, 8), lane8 // 8
    slot72 = lax.rem(lane72, 8)
    pyo[...] = jnp.zeros((XR, 128), F32)

    def newton(t, before):
        d, fx, fy = d_ref[t], fx_ref[t], fy_ref[t]
        q = fx * fx + fy * fy
        a = 1.0 + c_ref[t]
        m = (d + 0.5 * q) / (a + q)
        for _ in range(NEWTON - 1):
            s = m + 1.0
            s3 = s * s * s
            m = (d * s3 + q * (1.5 * s - 1.0)) / (a * s3 + q)
        shrink = m / (m + 1.0)
        vx, vy = fx * shrink, fy * shrink
        mass[t] = m
        px[t] = vx
        py[t] = vy
        b = m - before
        b = b + vx - jnp.where(row64 == 0, 0.0, roll(vx, 1, 0))
        b = b + vy - jnp.where(lane64 == 0, 0.0, roll(vy, 1, 1))
        eb[t + 2, 0:64, :] = b
        px0[pl.ds(t + 2, 1), :] = vx[63:64]
        pyo[0:64, :] = jnp.where(lane64 == 8 * t + 21, roll(vy, 8 * t + 22, 1), pyo[0:64, :])
        return m

    start = jnp.where(ta == 0, i_ref[...], 0.0)
    m7 = lax.fori_loop(0, 8, newton, start)

    for t in range(8):
        s_xp[2 * t : 2 * t + 2, :] = eb[t + 2, 62:64, :]
        s_xm[3 * t : 3 * t + 3, :] = eb[t + 2, 0:3, :]
    s_xp[16:24, :] = px0[2:10, :]
    s_xp[24:26, :] = m7[62:64]
    s_xp[26:28, :] = pyo[62:64, :]
    s_xm[24:27, :] = m7[0:3]
    s_xm[27:30, :] = pyo[0:3, :]
    s_pp[0:1, :] = eb[9, 63:64, :]
    s_pp[1:3, :] = px0[8:10, :]
    s_pp[3:5, :] = m7[62:64]
    s_pp[5:6, :] = pyo[63:64, :]
    s_pm[0:2, :] = eb[9, 0:2, :]
    s_pm[2:3, :] = eb[8, 0:1, :]
    s_pm[3:6, :] = m7[0:3]
    s_pm[6:8, :] = pyo[0:2, :]
    s_mp[0:2, :] = eb[2, 62:64, :]
    s_mp[2:3, :] = eb[3, 63:64, :]
    s_mp[3:6, :] = px0[2:5, :]
    s_mp[6:8, :] = pyo[62:64, :]
    s_mm[0:2, :] = eb[2, 0:2, :]
    s_mm[2:3, :] = eb[3, 0:1, :]
    s_mm[3:5, :] = pyo[0:2, :]

    def one(flag):
        return jnp.where(flag, 1, 0)

    greeted = len(ring_x + ring_y + ring_z) + 1 + 2 * one(has_p) + 2 * one(has_m)
    pl.semaphore_wait(bar, greeted + one(away_p) + one(away_m) + one(x == 3) + one(x == 0))

    def remote(i, src, dst, peer):
        return pltpu.make_async_remote_copy(
            src_ref=src, dst_ref=dst, send_sem=ss.at[i], recv_sem=rs.at[i],
            device_id=peer, device_id_type=MESH,
        )

    x_p = remote(0, s_xp, r_xm, at(0, gxp))
    x_m = remote(1, s_xm, r_xp, at(0, gxm))
    t_p = [
        remote(2, s_pp, r_mm, at(1, gxp)),
        remote(3, s_pm, r_mp, at(1, gxm)),
        remote(4, px0.at[8:10], px0.at[0:2], at(1, c["gx"])),
        remote(5, eb.at[8:10, 0:64], eb.at[0:2, 0:64], at(1, c["gx"])),
        remote(6, mass.at[7], mm.at[0:64], at(1, c["gx"])),
        remote(7, pyo.at[0:64], pyl.at[0:64], at(1, c["gx"])),
    ]
    t_m = [
        remote(8, s_mp, r_pm, at(-1, gxp)),
        remote(9, s_mm, r_pp, at(-1, gxm)),
        remote(10, px0.at[2:5], px0.at[10:13], at(-1, c["gx"])),
        remote(11, eb.at[2:5, 0:64], eb.at[10:13, 0:64], at(-1, c["gx"])),
        remote(12, pyo.at[0:64], pyh.at[0:64], at(-1, c["gx"])),
    ]

    @pl.when(has_p)
    def _():
        for copy in t_p[:2]:
            copy.start()

    @pl.when(has_m)
    def _():
        for copy in t_m[:2]:
            copy.start()

    x_p.start()
    x_m.start()

    @pl.when(has_m)
    def _():
        for copy in t_m[2:]:
            copy.start()

    @pl.when(has_p)
    def _():
        for copy in t_p[2:]:
            copy.start()

    for peer in ring_x + [mate]:
        pl.semaphore_signal(met, inc=1, device_id=peer, device_id_type=MESH)

    m0[0:64, :] = m7

    x_p.wait()
    x_m.wait()

    @pl.when(has_p)
    def _():
        for copy in t_p:
            copy.wait_send()

    @pl.when(has_m)
    def _():
        for copy in t_m:
            copy.wait_send()

    for t in range(8):
        eb[t + 2, 64:67, :] = r_xp[3 * t : 3 * t + 3, :]
        eb[t + 2, 70:72, :] = r_xm[2 * t : 2 * t + 2, :]
    pxm[2:10, :] = r_xm[16:24, :]
    m0[64:67, :] = r_xp[24:27, :]
    m0[70:72, :] = r_xm[24:26, :]
    pyo[64:67, :] = r_xp[27:30, :]
    pyo[70:72, :] = r_xm[26:28, :]

    @pl.when(has_m)
    def _():
        for copy in t_p:
            copy.wait_recv()
        eb[1, 71:72, :] = r_mm[0:1, :]
        pxm[0:2, :] = r_mm[1:3, :]
        mm[70:72, :] = r_mm[3:5, :]
        pyl[71:72, :] = r_mm[5:6, :]
        eb[1, 64:66, :] = r_mp[0:2, :]
        eb[0, 64:65, :] = r_mp[2:3, :]
        mm[64:67, :] = r_mp[3:6, :]
        pyl[64:66, :] = r_mp[6:8, :]
        eb[2] = eb[2] - mm[...]

    @pl.when(has_p)
    def _():
        for copy in t_m:
            copy.wait_recv()
        eb[10, 70:72, :] = r_pm[0:2, :]
        eb[11, 71:72, :] = r_pm[2:3, :]
        pxm[10:13, :] = r_pm[3:6, :]
        pyh[70:72, :] = r_pm[6:8, :]
        eb[10, 64:66, :] = r_pp[0:2, :]
        eb[11, 64:65, :] = r_pp[2:3, :]
        pyh[64:66, :] = r_pp[3:5, :]
        eb[10] = eb[10] - m0[...]

    for p in range(TP):
        eb[p, 0:1, :] = eb[p, 0:1, :] - pxm[p : p + 1, :]
        eb[p, 64:65, :] = eb[p, 64:65, :] - px0[p : p + 1, :]

    own = pyo[...]
    low = jnp.where(lane72 < 8, roll(own, 104, 1), roll(own, 120, 1))
    high = jnp.where(lane72 < 96, -roll(own, 16, 1), -roll(own, 32, 1))
    high = jnp.where(lane72 < 88, 0.0, high)
    low = jnp.where(has_m, roll(pyl[...], 64, 1), low)
    high = jnp.where(has_p, roll(pyh[...], 64, 1), high)
    py0 = jnp.where(lane72 < 16, low, jnp.where(lane72 < 80, own, high))

    @pl.when(jnp.logical_not(has_m))
    def _():
        eb[1] = eb[2]
        eb[0] = eb[3]

    @pl.when(jnp.logical_not(has_p))
    def _():
        eb[10] = jnp.zeros((XR, 128), F32)
        eb[11] = -eb[9]
        eb[12] = -eb[8]

    def pack(p, strips):
        v = eb[p]
        here = lane72 // 8 == p
        shifted = (roll(v, 8 * p + 2, 1), roll(v, 8 * p + 5, 1))
        return tuple(jnp.where(here, r, strip) for r, strip in zip(shifted, strips))

    zero8, zero72 = jnp.zeros((8, 128), F32), jnp.zeros((XR, 128), F32)
    left, right = zero72, zero72
    for p in range(TP):
        left, right = pack(p, (left, right))
    half = lax.rem(lax.broadcasted_iota(jnp.int32, (32, 128), 1), 8) < 4
    v = roll(jnp.where(slot72 == 5, py0, right), 125, 1)
    s_yp[0:32, :] = jnp.where(half, v[0:32], roll(v[40:72], 4, 1))
    s_yp[32:40, :] = v[32:40]
    v = roll(left, 3, 1)
    s_ym[0:32, :] = jnp.where(half, roll(v[40:72], 124, 1), v[0:32])
    s_ym[32:40, :] = v[32:40]
    y_p = remote(13, s_yp, r_ym, (ta, c["gx"], gyp))
    y_m = remote(14, s_ym, r_yp, (ta, c["gx"], gym))
    y_p.start()
    y_m.start()

    def spread(src, dst):
        def step(p, _):
            v = src[p]
            ends = roll(v, 1, 1) + roll(v, 127, 1)
            near = (src[p - 1] + src[p + 1]) + (roll(v, 1, 0) + roll(v, XR - 1, 0)) + ends
            dst[p] = 6.0 * v - near
            return 0

        return step

    def fold(v):
        return jnp.sum(v.reshape(8, 8, 128), axis=0)

    def shifted(b, u, w, k):
        v = u - k * SHIFT * b
        return v, (w - k * SHIFT * u) - k * SHIFT * v

    def edges(w, later):
        dx, dy = w - roll(w, XR - 1, 0), w - roll(w, 127, 1)
        dt, dx, dy = w[0:64] - later, dx[0:64], dy[0:64]
        return fold(dt * dt + dx * dx), fold(dy * dy)

    def moments(p, acc):
        here, nxt = (eb[p], e1[p], e2[p]), (eb[p + 1, 0:64, :], e1[p + 1, 0:64, :], e2[p + 1, 0:64, :])
        b = here[0][0:64]
        terms = [fold(b * b)]
        for k in range(SHIFTS):
            v, w = shifted(*here, k)
            e = edges(w, shifted(*nxt, k)[1])
            v, w = v[0:64], w[0:64]
            terms += [fold(b * v), fold(v * v), fold(v * w), fold(w * w), *e]
        return tuple(a + t for a, t in zip(acc, terms))

    for p in range(1, 12):
        spread(eb, e1)(p, 0)
    for p in range(2, 11):
        spread(e1, e2)(p, 0)
    acc = lax.fori_loop(2, 10, moments, (zero8,) * (1 + 6 * SHIFTS))

    y_p.wait()
    y_m.wait()
    v = r_ym[...]
    near = jnp.concatenate([v, roll(v[0:32], 124, 1)], 0)
    left = jnp.where(slot72 < 2, near, left) - jnp.where(slot72 == 2, near, 0.0)
    v = r_yp[...]
    near = jnp.concatenate([v, roll(v[0:32], 4, 1)], 0)
    right = jnp.where(slot72 >= 5, near, right) - jnp.where(slot72 == 5, py0, 0.0)

    def apply(v):
        return 6.0 * v - (
            (roll(v, 8, 1) + roll(v, 120, 1))
            + (roll(v, 1, 0) + roll(v, XR - 1, 0))
            + (roll(v, 1, 1) + roll(v, 127, 1))
        )

    inner = jnp.logical_and(lane8 >= 3, lane8 < 126)
    inner_y = jnp.logical_and(lane8 >= 3, lane8 < 125)
    masks = [inner] + ([inner] * 5 + [inner_y]) * SHIFTS
    acc = [jnp.where(mask, v, 0.0) for mask, v in zip(masks, acc)]
    block = jnp.logical_and(plane8 >= 2, plane8 < 10)
    pairs = jnp.logical_and(block, jnp.logical_and(slot8 >= 2, slot8 < 5))
    strips = []
    for b, lo in ((left, 2), (right, 3)):
        u = apply(b)
        strips.append((b, u, apply(u)))
        cells = jnp.logical_and(block, jnp.logical_and(slot8 >= lo, slot8 < 5))
        b64 = b[0:64]
        terms = [fold(b64 * b64)]
        for k in range(SHIFTS):
            v, w = shifted(*strips[-1], k)
            e = edges(w, roll(w, 120, 1)[0:64])
            v, w = v[0:64], w[0:64]
            terms += [fold(b64 * v), fold(v * v), fold(v * w), fold(w * w), *e]
        masks = [cells] + ([cells] * 5 + [pairs]) * SHIFTS
        acc = [a + jnp.where(mask, e, 0.0) for a, mask, e in zip(acc, masks, terms)]
    sub8 = lax.broadcasted_iota(jnp.int32, (8, 128), 0)
    spot = zero8
    for j in range(6):
        rows = zero8
        for k in range(SHIFTS):
            v = acc[0] if j == 0 else acc[6 * k + j]
            if j == 5:
                v = v + acc[6 * k + 6]
            rows = jnp.where(sub8 == k, jnp.sum(v, axis=0, keepdims=True), rows)
        spot = jnp.where(lane8 == 8 * j + sub8, jnp.sum(rows, axis=1, keepdims=True), spot)
    row = jnp.sum(spot, axis=0, keepdims=True)

    def send_all(buf, row, peers, send, recv):
        n = len(peers)
        buf[0] = row
        for i, peer in enumerate(peers):
            pltpu.make_async_remote_copy(
                src_ref=buf.at[0], dst_ref=buf.at[i + 1], send_sem=send, recv_sem=recv,
                device_id=peer, device_id_type=MESH,
            ).start()
        return pltpu.make_async_remote_copy(
            src_ref=buf.at[1 : n + 1], dst_ref=buf.at[1 : n + 1], send_sem=send, recv_sem=recv,
            device_id=peers[0], device_id_type=MESH,
        )

    def sum_all(buf, n):
        total = buf[0]
        for i in range(n):
            total = total + buf[i + 1]
        return total

    pl.semaphore_wait(met, len(ring_x) + 1)
    sent_a = send_all(buf_a, row, peers_a, ra_send, ra_recv)

    def differences(i, e):
        sl, sr = strips[0][i], strips[1][i]

        def whole(p):
            v = jnp.where(lane72 < 3, roll(sl, 126 - 8 * p, 1), e[p])
            return jnp.where(lane72 >= 126, roll(sr, 123 - 8 * p, 1), v)

        def step(t, v):
            p = t + 2
            nxt = whole(p + 1)
            v64 = v[0:64]
            hi = roll(jnp.where(lane64 == 0, roll(sr[0:64], 123 - 8 * p, 1), v64), 127, 1)
            diffs[i, 0, t] = v64 - nxt[0:64]
            diffs[i, 1, t] = v64 - roll(v, XR - 1, 0)[0:64]
            diffs[i, 2, t] = v64 - hi
            return nxt

        lax.fori_loop(0, 8, step, whole(2))

    for i, e in enumerate((eb, e1, e2)):
        differences(i, e)

    sent_a.wait_recv()
    row = sum_all(buf_a, len(peers_a))
    sent_b = send_all(buf_b, row, peers_b, rb_send, rb_recv)
    sent_b.wait_recv()
    row = sum_all(buf_b, len(peers_b))
    row = jnp.broadcast_to(row, (8, 128))
    m0, m1, m2, m3, m4, g4 = (row if j == 0 else roll(row, 128 - 8 * j, 1) for j in range(6))
    shift = SHIFT * lane8.astype(F32)
    g0, g1, g2, g3 = shift * m0 + m1, shift * m1 + m2, shift * m2 + m3, shift * m3 + m4
    l1, l2 = g1 / g0, g2 / g0
    d1 = g2 - l1 * g1
    f1 = g3 - l2 * g1
    i1 = jnp.where(d1 > 0.0, 1.0 / d1, 0.0)
    l3 = f1 * i1
    d2 = g4 - l2 * g2 - l3 * f1
    y1 = m1 - l1 * m0
    y2 = m2 - l2 * m0 - l3 * y1
    c2 = jnp.where(d2 > 0.0, y2 / d2, 0.0)
    c1 = y1 * i1 - l3 * c2
    c0 = m0 / g0 - l1 * c1 - l2 * c2
    c0, c1 = c0 - shift * (c1 - shift * c2), c1 - 2.0 * shift * c2
    far = jnp.where(lane8 < SHIFTS, jnp.abs(m1), jnp.inf)
    best = far == jnp.min(far, axis=1, keepdims=True)
    count = jnp.sum(jnp.where(best, 1.0, 0.0), axis=1, keepdims=True)
    c0, c1, c2 = (
        jnp.sum(jnp.where(best, v, 0.0), axis=1, keepdims=True) / count for v in (c0, c1, c2)
    )
    for i, v in enumerate((c0, c1, c2)):
        coef[i] = jnp.broadcast_to(v, (8, 128))
    sent_a.wait_send()
    sent_b.wait_send()


def store(m_ref, x_ref, y_ref, diffs, coef, m_out, x_out, y_out, m_buf, x_buf, y_buf, sem):
    c0, c1, c2 = (jnp.concatenate([coef[i]] * 8, 0) for i in range(3))
    copies = []
    for k, (old, buf, out) in enumerate(
        ((m_ref, m_buf, m_out), (x_ref, x_buf, x_out), (y_ref, y_buf, y_out))
    ):

        def plane(t, _, k=k, old=old, buf=buf):
            step = c0 * diffs[0, k, t] + c1 * diffs[1, k, t] + c2 * diffs[2, k, t]
            buf[t] = old[t] - step
            return 0

        lax.fori_loop(0, 8, plane, 0)
        copies.append(pltpu.make_async_copy(buf, out, sem.at[k]))
        copies[k].start()
    for copy in copies:
        copy.wait()


def body(density, flux_x, flux_y, congestion, initial_density):
    block = jax.ShapeDtypeStruct((8, 64, 128), F32)
    vm = lambda *s: pltpu.VMEM(s, F32)
    dma = pltpu.SemaphoreType.DMA
    arrays = (density, flux_x, flux_y, congestion, initial_density)
    arrays = [pltpu.with_memory_space_constraint(a, pltpu.HBM) for a in arrays]
    outs = pl.pallas_call(
        kernel,
        out_shape=(block,) * 3 + tuple(
            jax.ShapeDtypeStruct(shape, F32) for shape in ((3, 3, 8, 64, 128), (3, 8, 128))
        ),
        in_specs=[pl.BlockSpec(memory_space=pltpu.HBM)] * 5,
        out_specs=[pl.BlockSpec(memory_space=pltpu.VMEM)] * 5,
        scratch_shapes=[vm(8, 64, 128)] * 4
        + [vm(64, 128)]
        + [vm(TP, XR, 128)] * 3
        + [vm(16, 128)] * 2
        + [vm(XR, 128)] * 5
        + [vm(32, 128)] * 2
        + [vm(8, 128)] * 4
        + [vm(32, 128)] * 2
        + [vm(8, 128)] * 4
        + [vm(40, 128)] * 4
        + [vm(16, 1, 128), vm(32, 1, 128)]
        + [dma((5,)), dma((15,)), dma((15,))]
        + [dma] * 4
        + [pltpu.SemaphoreType.REGULAR],
        compiler_params=pltpu.CompilerParams(
            collective_id=0, has_side_effects=True, vmem_limit_bytes=VMEM_MAIN
        ),
        name="prox_project",
    )(*arrays)
    return pl.pallas_call(
        store,
        out_shape=(block,) * 3,
        in_specs=[pl.BlockSpec(memory_space=pltpu.VMEM)] * 5,
        out_specs=[pl.BlockSpec(memory_space=pltpu.HBM)] * 3,
        scratch_shapes=[vm(8, 64, 128)] * 3 + [dma((3,))],
        compiler_params=pltpu.CompilerParams(vmem_limit_bytes=VMEM_STORE),
        name="store",
    )(*outs)


def solution(mesh):
    spec = P("ta", "gx", "gy")
    return jax.shard_map(
        body,
        mesh=mesh,
        in_specs=(spec,) * 4 + (P("gx", "gy"),),
        out_specs=(spec,) * 3,
        check_vma=False,
    )
```

```python
import functools
import itertools

import jax
import jax.numpy as jnp
from jax import lax
from jax.experimental import pallas as pl
from jax.experimental.pallas import tpu as pltpu
from jax.sharding import PartitionSpec as P

MESH = pl.DeviceIdType.MESH
NEWTON = 6
F32 = jnp.float32
TP, XR = 13, 72
SHIFT, SHIFTS = 4.0, 4
VMEM_MAIN, VMEM_STORE = 16 * 2**20, 4 * 2**20


def roll(v, shift, axis):
    return pltpu.roll(v, shift, axis)


def group_a(c):
    peers = []
    for dz, dc in itertools.product(range(8), range(2)):
        if dz or dc:
            ta = c["ta"] + dc * (1 - 2 * lax.rem(c["ta"], 2))
            peers.append((min(dz, 8 - dz), (ta, c["gx"], lax.rem(c["gy"] + dz, 8))))
    return [p for _, p in sorted(peers, key=lambda e: -e[0])]


def group_b(c):
    y, x = (c["gx"] // 4) * 4 + c["ta"] // 2, lax.rem(c["gx"], 4)
    peers = []
    for dy, dx in itertools.product(range(8), range(4)):
        if dy or dx:
            yy, xx = lax.rem(y + dy, 8), lax.rem(x + dx, 4)
            at = (lax.rem(yy, 4) * 2 + lax.rem(c["ta"], 2), (yy // 4) * 4 + xx, c["gy"])
            peers.append((min(dy, 8 - dy) + min(dx, 4 - dx), at))
    return [p for _, p in sorted(peers, key=lambda e: -e[0])]


def kernel(
    d_hbm, fx_hbm, fy_hbm, c_hbm, i_hbm,
    mass, px, py, diffs, coef,
    d_ref, fx_ref, fy_ref, c_ref, i_ref,
    eb, e1, e2, px0, pxm, m0, mm, pyo, pyl, pyh,
    s_xp, s_xm, s_pp, s_pm, s_mp, s_mm,
    r_xm, r_xp, r_mm, r_mp, r_pm, r_pp,
    s_yp, s_ym, r_ym, r_yp, buf_a, buf_b,
    in_sem, ss, rs, ra_send, ra_recv, rb_send, rb_recv, met,
):
    c = {a: lax.axis_index(a) for a in ("ta", "gx", "gy")}
    ta = c["ta"]
    has_m, has_p = ta > 0, ta < 7
    gxp, gxm = lax.rem(c["gx"] + 1, 8), lax.rem(c["gx"] + 7, 8)
    gyp, gym = lax.rem(c["gy"] + 1, 8), lax.rem(c["gy"] + 7, 8)
    peers_a, peers_b = group_a(c), group_b(c)

    def at(dt, gx):
        return (ta + dt, gx, c["gy"])

    bar = pltpu.get_barrier_semaphore()

    def greet(peer):
        pl.semaphore_signal(bar, inc=1, device_id=peer, device_id_type=MESH)

    core, x, y = lax.rem(ta, 2), lax.rem(c["gx"], 4), (c["gx"] // 4) * 4 + ta // 2
    odd = core == 1
    away_p = jnp.logical_and(has_p, odd)
    away_m = jnp.logical_and(has_m, jnp.logical_not(odd))
    mate = at(1 - 2 * core, c["gx"])
    ring_x = [at(0, (c["gx"] // 4) * 4 + lax.rem(x + d, 4)) for d in (2, 1, 3)]
    ring_z = [(ta, c["gx"], lax.rem(c["gy"] + d, 8)) for d in (4, 3, 5, 2, 6, 1, 7)]
    ring_y = []
    for d in (4, 3, 5, 2, 6, 1, 7):
        yy = lax.rem(y + d, 8)
        ring_y.append((lax.rem(yy, 4) * 2 + core, (yy // 4) * 4 + x, c["gy"]))

    @pl.when(has_p)
    def _():
        greet(at(1, gxp))
        greet(at(1, gxm))

    @pl.when(has_m)
    def _():
        greet(at(-1, gxp))
        greet(at(-1, gxm))

    @pl.when(x == 3)
    def _():
        greet(at(0, gxp))

    @pl.when(x == 0)
    def _():
        greet(at(0, gxm))

    loads = [
        pltpu.make_async_copy(a, b, in_sem.at[i])
        for i, (a, b) in enumerate(
            ((d_hbm, d_ref), (fx_hbm, fx_ref), (fy_hbm, fy_ref), (c_hbm, c_ref), (i_hbm, i_ref))
        )
    ]
    for copy in loads:
        copy.start()

    for peer in ring_y + ring_z + ring_x:
        greet(peer)

    @pl.when(away_p)
    def _():
        greet(at(1, c["gx"]))

    @pl.when(away_m)
    def _():
        greet(at(-1, c["gx"]))

    greet(mate)

    for copy in loads:
        copy.wait()

    lane64 = lax.broadcasted_iota(jnp.int32, (64, 128), 1)
    row64 = lax.broadcasted_iota(jnp.int32, (64, 128), 0)
    lane8 = lax.broadcasted_iota(jnp.int32, (8, 128), 1)
    lane72 = lax.broadcasted_iota(jnp.int32, (XR, 128), 1)
    slot8, plane8 = lax.rem(lane8, 8), lane8 // 8
    slot72 = lax.rem(lane72, 8)
    pyo[...] = jnp.zeros((XR, 128), F32)

    def newton(t, before):
        d, fx, fy = d_ref[t], fx_ref[t], fy_ref[t]
        q = fx * fx + fy * fy
        a = 1.0 + c_ref[t]
        m = (d + 0.5 * q) / (a + q)
        for _ in range(NEWTON - 1):
            s = m + 1.0
            s3 = s * s * s
            m = (d * s3 + q * (1.5 * s - 1.0)) / (a * s3 + q)
        shrink = m / (m + 1.0)
        vx, vy = fx * shrink, fy * shrink
        mass[t] = m
        px[t] = vx
        py[t] = vy
        b = m - before
        b = b + vx - jnp.where(row64 == 0, 0.0, roll(vx, 1, 0))
        b = b + vy - jnp.where(lane64 == 0, 0.0, roll(vy, 1, 1))
        eb[t + 2, 0:64, :] = b
        px0[pl.ds(t + 2, 1), :] = vx[63:64]
        pyo[0:64, :] = jnp.where(lane64 == 8 * t + 21, roll(vy, 8 * t + 22, 1), pyo[0:64, :])
        return m

    start = jnp.where(ta == 0, i_ref[...], 0.0)
    m7 = lax.fori_loop(0, 8, newton, start)

    for t in range(8):
        s_xp[2 * t : 2 * t + 2, :] = eb[t + 2, 62:64, :]
        s_xm[3 * t : 3 * t + 3, :] = eb[t + 2, 0:3, :]
    s_xp[16:24, :] = px0[2:10, :]
    s_xp[24:26, :] = m7[62:64]
    s_xp[26:28, :] = pyo[62:64, :]
    s_xm[24:27, :] = m7[0:3]
    s_xm[27:30, :] = pyo[0:3, :]
    s_pp[0:1, :] = eb[9, 63:64, :]
    s_pp[1:3, :] = px0[8:10, :]
    s_pp[3:5, :] = m7[62:64]
    s_pp[5:6, :] = pyo[63:64, :]
    s_pm[0:2, :] = eb[9, 0:2, :]
    s_pm[2:3, :] = eb[8, 0:1, :]
    s_pm[3:6, :] = m7[0:3]
    s_pm[6:8, :] = pyo[0:2, :]
    s_mp[0:2, :] = eb[2, 62:64, :]
    s_mp[2:3, :] = eb[3, 63:64, :]
    s_mp[3:6, :] = px0[2:5, :]
    s_mp[6:8, :] = pyo[62:64, :]
    s_mm[0:2, :] = eb[2, 0:2, :]
    s_mm[2:3, :] = eb[3, 0:1, :]
    s_mm[3:5, :] = pyo[0:2, :]

    def one(flag):
        return jnp.where(flag, 1, 0)

    greeted = len(ring_x + ring_y + ring_z) + 1 + 2 * one(has_p) + 2 * one(has_m)
    pl.semaphore_wait(bar, greeted + one(away_p) + one(away_m) + one(x == 3) + one(x == 0))

    def remote(i, src, dst, peer):
        return pltpu.make_async_remote_copy(
            src_ref=src, dst_ref=dst, send_sem=ss.at[i], recv_sem=rs.at[i],
            device_id=peer, device_id_type=MESH,
        )

    x_p = remote(0, s_xp, r_xm, at(0, gxp))
    x_m = remote(1, s_xm, r_xp, at(0, gxm))
    t_p = [
        remote(2, s_pp, r_mm, at(1, gxp)),
        remote(3, s_pm, r_mp, at(1, gxm)),
        remote(4, px0.at[8:10], px0.at[0:2], at(1, c["gx"])),
        remote(5, eb.at[8:10, 0:64], eb.at[0:2, 0:64], at(1, c["gx"])),
        remote(6, mass.at[7], mm.at[0:64], at(1, c["gx"])),
        remote(7, pyo.at[0:64], pyl.at[0:64], at(1, c["gx"])),
    ]
    t_m = [
        remote(8, s_mp, r_pm, at(-1, gxp)),
        remote(9, s_mm, r_pp, at(-1, gxm)),
        remote(10, px0.at[2:5], px0.at[10:13], at(-1, c["gx"])),
        remote(11, eb.at[2:5, 0:64], eb.at[10:13, 0:64], at(-1, c["gx"])),
        remote(12, pyo.at[0:64], pyh.at[0:64], at(-1, c["gx"])),
    ]

    @pl.when(has_p)
    def _():
        for copy in t_p[:2]:
            copy.start()

    @pl.when(has_m)
    def _():
        for copy in t_m[:2]:
            copy.start()

    x_p.start()
    x_m.start()

    @pl.when(has_m)
    def _():
        for copy in t_m[2:]:
            copy.start()

    @pl.when(has_p)
    def _():
        for copy in t_p[2:]:
            copy.start()

    for peer in ring_x + [mate]:
        pl.semaphore_signal(met, inc=1, device_id=peer, device_id_type=MESH)

    m0[0:64, :] = m7

    x_p.wait()
    x_m.wait()

    @pl.when(has_p)
    def _():
        for copy in t_p:
            copy.wait_send()

    @pl.when(has_m)
    def _():
        for copy in t_m:
            copy.wait_send()

    for t in range(8):
        eb[t + 2, 64:67, :] = r_xp[3 * t : 3 * t + 3, :]
        eb[t + 2, 70:72, :] = r_xm[2 * t : 2 * t + 2, :]
    pxm[2:10, :] = r_xm[16:24, :]
    m0[64:67, :] = r_xp[24:27, :]
    m0[70:72, :] = r_xm[24:26, :]
    pyo[64:67, :] = r_xp[27:30, :]
    pyo[70:72, :] = r_xm[26:28, :]

    @pl.when(has_m)
    def _():
        for copy in t_p:
            copy.wait_recv()
        eb[1, 71:72, :] = r_mm[0:1, :]
        pxm[0:2, :] = r_mm[1:3, :]
        mm[70:72, :] = r_mm[3:5, :]
        pyl[71:72, :] = r_mm[5:6, :]
        eb[1, 64:66, :] = r_mp[0:2, :]
        eb[0, 64:65, :] = r_mp[2:3, :]
        mm[64:67, :] = r_mp[3:6, :]
        pyl[64:66, :] = r_mp[6:8, :]
        eb[2] = eb[2] - mm[...]

    @pl.when(has_p)
    def _():
        for copy in t_m:
            copy.wait_recv()
        eb[10, 70:72, :] = r_pm[0:2, :]
        eb[11, 71:72, :] = r_pm[2:3, :]
        pxm[10:13, :] = r_pm[3:6, :]
        pyh[70:72, :] = r_pm[6:8, :]
        eb[10, 64:66, :] = r_pp[0:2, :]
        eb[11, 64:65, :] = r_pp[2:3, :]
        pyh[64:66, :] = r_pp[3:5, :]
        eb[10] = eb[10] - m0[...]

    for p in range(TP):
        eb[p, 0:1, :] = eb[p, 0:1, :] - pxm[p : p + 1, :]
        eb[p, 64:65, :] = eb[p, 64:65, :] - px0[p : p + 1, :]

    own = pyo[...]
    low = jnp.where(lane72 < 8, roll(own, 104, 1), roll(own, 120, 1))
    high = jnp.where(lane72 < 96, -roll(own, 16, 1), -roll(own, 32, 1))
    high = jnp.where(lane72 < 88, 0.0, high)
    low = jnp.where(has_m, roll(pyl[...], 64, 1), low)
    high = jnp.where(has_p, roll(pyh[...], 64, 1), high)
    py0 = jnp.where(lane72 < 16, low, jnp.where(lane72 < 80, own, high))

    @pl.when(jnp.logical_not(has_m))
    def _():
        eb[1] = eb[2]
        eb[0] = eb[3]

    @pl.when(jnp.logical_not(has_p))
    def _():
        eb[10] = jnp.zeros((XR, 128), F32)
        eb[11] = -eb[9]
        eb[12] = -eb[8]

    def pack(p, strips):
        v = eb[p]
        here = lane72 // 8 == p
        shifted = (roll(v, 8 * p + 2, 1), roll(v, 8 * p + 5, 1))
        return tuple(jnp.where(here, r, strip) for r, strip in zip(shifted, strips))

    zero8, zero72 = jnp.zeros((8, 128), F32), jnp.zeros((XR, 128), F32)
    left, right = zero72, zero72
    for p in range(TP):
        left, right = pack(p, (left, right))
    half = lax.rem(lax.broadcasted_iota(jnp.int32, (32, 128), 1), 8) < 4
    v = roll(jnp.where(slot72 == 5, py0, right), 125, 1)
    s_yp[0:32, :] = jnp.where(half, v[0:32], roll(v[40:72], 4, 1))
    s_yp[32:40, :] = v[32:40]
    v = roll(left, 3, 1)
    s_ym[0:32, :] = jnp.where(half, roll(v[40:72], 124, 1), v[0:32])
    s_ym[32:40, :] = v[32:40]
    y_p = remote(13, s_yp, r_ym, (ta, c["gx"], gyp))
    y_m = remote(14, s_ym, r_yp, (ta, c["gx"], gym))
    y_p.start()
    y_m.start()

    def spread(src, dst):
        def step(p, _):
            v = src[p]
            ends = roll(v, 1, 1) + roll(v, 127, 1)
            near = (src[p - 1] + src[p + 1]) + (roll(v, 1, 0) + roll(v, XR - 1, 0)) + ends
            dst[p] = 6.0 * v - near
            return 0

        return step

    def fold(v):
        return jnp.sum(v.reshape(8, 8, 128), axis=0)

    def shifted(b, u, w, k):
        v = u - k * SHIFT * b
        return v, (w - k * SHIFT * u) - k * SHIFT * v

    def edges(w, later):
        dx, dy = w - roll(w, XR - 1, 0), w - roll(w, 127, 1)
        dt, dx, dy = w[0:64] - later, dx[0:64], dy[0:64]
        return fold(dt * dt + dx * dx), fold(dy * dy)

    def moments(p, acc):
        here, nxt = (eb[p], e1[p], e2[p]), (eb[p + 1, 0:64, :], e1[p + 1, 0:64, :], e2[p + 1, 0:64, :])
        b = here[0][0:64]
        terms = [fold(b * b)]
        for k in range(SHIFTS):
            v, w = shifted(*here, k)
            e = edges(w, shifted(*nxt, k)[1])
            v, w = v[0:64], w[0:64]
            terms += [fold(b * v), fold(v * v), fold(v * w), fold(w * w), *e]
        return tuple(a + t for a, t in zip(acc, terms))

    for p in range(1, 12):
        spread(eb, e1)(p, 0)
    for p in range(2, 11):
        spread(e1, e2)(p, 0)
    acc = lax.fori_loop(2, 10, moments, (zero8,) * (1 + 6 * SHIFTS))

    y_p.wait()
    y_m.wait()
    v = r_ym[...]
    near = jnp.concatenate([v, roll(v[0:32], 124, 1)], 0)
    left = jnp.where(slot72 < 2, near, left) - jnp.where(slot72 == 2, near, 0.0)
    v = r_yp[...]
    near = jnp.concatenate([v, roll(v[0:32], 4, 1)], 0)
    right = jnp.where(slot72 >= 5, near, right) - jnp.where(slot72 == 5, py0, 0.0)

    def apply(v):
        return 6.0 * v - (
            (roll(v, 8, 1) + roll(v, 120, 1))
            + (roll(v, 1, 0) + roll(v, XR - 1, 0))
            + (roll(v, 1, 1) + roll(v, 127, 1))
        )

    inner = jnp.logical_and(lane8 >= 3, lane8 < 126)
    inner_y = jnp.logical_and(lane8 >= 3, lane8 < 125)
    masks = [inner] + ([inner] * 5 + [inner_y]) * SHIFTS
    acc = [jnp.where(mask, v, 0.0) for mask, v in zip(masks, acc)]
    block = jnp.logical_and(plane8 >= 2, plane8 < 10)
    pairs = jnp.logical_and(block, jnp.logical_and(slot8 >= 2, slot8 < 5))
    strips = []
    for b, lo in ((left, 2), (right, 3)):
        u = apply(b)
        strips.append((b, u, apply(u)))
        cells = jnp.logical_and(block, jnp.logical_and(slot8 >= lo, slot8 < 5))
        b64 = b[0:64]
        terms = [fold(b64 * b64)]
        for k in range(SHIFTS):
            v, w = shifted(*strips[-1], k)
            e = edges(w, roll(w, 120, 1)[0:64])
            v, w = v[0:64], w[0:64]
            terms += [fold(b64 * v), fold(v * v), fold(v * w), fold(w * w), *e]
        masks = [cells] + ([cells] * 5 + [pairs]) * SHIFTS
        acc = [a + jnp.where(mask, e, 0.0) for a, mask, e in zip(acc, masks, terms)]
    sub8 = lax.broadcasted_iota(jnp.int32, (8, 128), 0)
    spot = zero8
    for j in range(6):
        rows = zero8
        for k in range(SHIFTS):
            v = acc[0] if j == 0 else acc[6 * k + j]
            if j == 5:
                v = v + acc[6 * k + 6]
            rows = jnp.where(sub8 == k, jnp.sum(v, axis=0, keepdims=True), rows)
        spot = jnp.where(lane8 == 8 * j + sub8, jnp.sum(rows, axis=1, keepdims=True), spot)
    row = jnp.sum(spot, axis=0, keepdims=True)

    def send_all(buf, row, peers, send, recv):
        n = len(peers)
        buf[0] = row
        for i, peer in enumerate(peers):
            pltpu.make_async_remote_copy(
                src_ref=buf.at[0], dst_ref=buf.at[i + 1], send_sem=send, recv_sem=recv,
                device_id=peer, device_id_type=MESH,
            ).start()
        return pltpu.make_async_remote_copy(
            src_ref=buf.at[1 : n + 1], dst_ref=buf.at[1 : n + 1], send_sem=send, recv_sem=recv,
            device_id=peers[0], device_id_type=MESH,
        )

    def sum_all(buf, n):
        total = buf[0]
        for i in range(n):
            total = total + buf[i + 1]
        return total

    pl.semaphore_wait(met, len(ring_x) + 1)
    sent_a = send_all(buf_a, row, peers_a, ra_send, ra_recv)

    def differences(i, e):
        sl, sr = strips[0][i], strips[1][i]

        def whole(p):
            v = jnp.where(lane72 < 3, roll(sl, 126 - 8 * p, 1), e[p])
            return jnp.where(lane72 >= 126, roll(sr, 123 - 8 * p, 1), v)

        def step(t, v):
            p = t + 2
            nxt = whole(p + 1)
            v64 = v[0:64]
            hi = roll(jnp.where(lane64 == 0, roll(sr[0:64], 123 - 8 * p, 1), v64), 127, 1)
            diffs[i, 0, t] = v64 - nxt[0:64]
            diffs[i, 1, t] = v64 - roll(v, XR - 1, 0)[0:64]
            diffs[i, 2, t] = v64 - hi
            return nxt

        lax.fori_loop(0, 8, step, whole(2))

    for i, e in enumerate((eb, e1, e2)):
        differences(i, e)

    sent_a.wait_recv()
    row = sum_all(buf_a, len(peers_a))
    sent_b = send_all(buf_b, row, peers_b, rb_send, rb_recv)
    sent_b.wait_recv()
    row = sum_all(buf_b, len(peers_b))
    row = jnp.broadcast_to(row, (8, 128))
    m0, m1, m2, m3, m4, g4 = (row if j == 0 else roll(row, 128 - 8 * j, 1) for j in range(6))
    shift = SHIFT * lane8.astype(F32)
    g0, g1, g2, g3 = shift * m0 + m1, shift * m1 + m2, shift * m2 + m3, shift * m3 + m4
    l1, l2 = g1 / g0, g2 / g0
    d1 = g2 - l1 * g1
    f1 = g3 - l2 * g1
    i1 = jnp.where(d1 > 0.0, 1.0 / d1, 0.0)
    l3 = f1 * i1
    d2 = g4 - l2 * g2 - l3 * f1
    y1 = m1 - l1 * m0
    y2 = m2 - l2 * m0 - l3 * y1
    c2 = jnp.where(d2 > 0.0, y2 / d2, 0.0)
    c1 = y1 * i1 - l3 * c2
    c0 = m0 / g0 - l1 * c1 - l2 * c2
    c0, c1 = c0 - shift * (c1 - shift * c2), c1 - 2.0 * shift * c2
    far = jnp.where(lane8 < SHIFTS, jnp.abs(m1), jnp.inf)
    best = far == jnp.min(far, axis=1, keepdims=True)
    count = jnp.sum(jnp.where(best, 1.0, 0.0), axis=1, keepdims=True)
    c0, c1, c2 = (
        jnp.sum(jnp.where(best, v, 0.0), axis=1, keepdims=True) / count for v in (c0, c1, c2)
    )
    for i, v in enumerate((c0, c1, c2)):
        coef[i] = jnp.broadcast_to(v, (8, 128))
    sent_a.wait_send()
    sent_b.wait_send()


def store(m_ref, x_ref, y_ref, diffs, coef, m_out, x_out, y_out, m_buf, x_buf, y_buf, sem):
    c0, c1, c2 = (jnp.concatenate([coef[i]] * 8, 0) for i in range(3))
    copies = []
    for k, (old, buf, out) in enumerate(
        ((m_ref, m_buf, m_out), (x_ref, x_buf, x_out), (y_ref, y_buf, y_out))
    ):

        def plane(t, _, k=k, old=old, buf=buf):
            step = c0 * diffs[0, k, t] + c1 * diffs[1, k, t] + c2 * diffs[2, k, t]
            buf[t] = old[t] - step
            return 0

        for h in (0, 4):
            lax.fori_loop(h, h + 4, plane, 0)
            copy = pltpu.make_async_copy(buf.at[h : h + 4], out.at[h : h + 4], sem.at[k, h // 4])
            copy.start()
            copies.append(copy)
    for copy in copies:
        copy.wait()


def body(density, flux_x, flux_y, congestion, initial_density):
    block = jax.ShapeDtypeStruct((8, 64, 128), F32)
    vm = lambda *s: pltpu.VMEM(s, F32)
    dma = pltpu.SemaphoreType.DMA
    arrays = (density, flux_x, flux_y, congestion, initial_density)
    arrays = [pltpu.with_memory_space_constraint(a, pltpu.HBM) for a in arrays]
    outs = pl.pallas_call(
        kernel,
        out_shape=(block,) * 3 + tuple(
            jax.ShapeDtypeStruct(shape, F32) for shape in ((3, 3, 8, 64, 128), (3, 8, 128))
        ),
        in_specs=[pl.BlockSpec(memory_space=pltpu.HBM)] * 5,
        out_specs=[pl.BlockSpec(memory_space=pltpu.VMEM)] * 5,
        scratch_shapes=[vm(8, 64, 128)] * 4
        + [vm(64, 128)]
        + [vm(TP, XR, 128)] * 3
        + [vm(16, 128)] * 2
        + [vm(XR, 128)] * 5
        + [vm(32, 128)] * 2
        + [vm(8, 128)] * 4
        + [vm(32, 128)] * 2
        + [vm(8, 128)] * 4
        + [vm(40, 128)] * 4
        + [vm(16, 1, 128), vm(32, 1, 128)]
        + [dma((5,)), dma((15,)), dma((15,))]
        + [dma] * 4
        + [pltpu.SemaphoreType.REGULAR],
        compiler_params=pltpu.CompilerParams(
            collective_id=0, has_side_effects=True, vmem_limit_bytes=VMEM_MAIN
        ),
        name="prox_project",
    )(*arrays)
    return pl.pallas_call(
        store,
        out_shape=(block,) * 3,
        in_specs=[pl.BlockSpec(memory_space=pltpu.VMEM)] * 5,
        out_specs=[pl.BlockSpec(memory_space=pltpu.HBM)] * 3,
        scratch_shapes=[vm(8, 64, 128)] * 3 + [dma((3, 2))],
        compiler_params=pltpu.CompilerParams(vmem_limit_bytes=VMEM_STORE),
        name="store",
    )(*outs)


def solution(mesh):
    spec = P("ta", "gx", "gy")
    return jax.shard_map(
        body,
        mesh=mesh,
        in_specs=(spec,) * 4 + (P("gx", "gy"),),
        out_specs=(spec,) * 3,
        check_vma=False,
    )
```
